1024 devices in a mesh: gx: 32 (over y, z_lo), gz: 32 (over x, z_hi, core).
Axes of the slice: x: 4, y: 8, z: 16 (z_hi: 4, z_lo: 4; z = z_hi * 4 + z_lo), core: 2. Of those that a mesh axis runs over, the one named last changes fastest.
Arguments:
- populations: float32 [19, 128, 512, 128], P(None, 'gx', 'gz'), may hold values from 0.019 to 0.44, as said below
- fluid_mask: int32 [128, 512, 128], P('gx', 'gz'), may hold values 0 or 1
Outputs:
- spectrum: float32 [2, 128, 128, 512], P(None, 'gx', 'gz')
The draws below stay inside these ranges and needn't reach their ends.
Inputs may be any that keep to these rules, and one draw needn't show every extreme that they name: `populations`: each entry lies between 0.7 and 1.3 times the weight of its velocity.
All inputs are finite; a program needn't handle non-finite values. No bound on the sum of `fluid_mask` on one device may be relied on, other than what follows from the above.
Results may differ from the reference program's by a relative error of at most 0.0003.
Values sent between devices are 32-bit elements; how exact they have to be, the bound alone decides.
No kernel may reach another device: no remote copies, remote signals or barrier semaphores. Data moves between devices by JAX's collectives and lax.ppermute only.
A program may use at most 32 MiB of HBM per device.

```python
import math
import jax
import jax.numpy as jnp
from jax import lax

NY = 128
NX = 128
NZ = 512


LATTICE_WEIGHTS = (1.0 / 3.0,) + (1.0 / 18.0,) * 6 + (1.0 / 36.0,) * 12


def draw_populations(key, part):
    weights = jnp.asarray(LATTICE_WEIGHTS, jnp.float32).reshape(19, 1, 1, 1)
    shape = (19, NX, NZ, NY)
    noise = jnp.clip(jax.random.normal(key, shape, jnp.float32), -3.0, 3.0)
    factor = 1.0 + 0.1 * noise
    return weights * factor


def plant(entries, stream_key, least, top_value):
    place = [jax.random.randint(jax.random.fold_in(stream_key, axis), (), 0, length) for axis, length in enumerate(entries.shape)]
    widest = entries.shape.index(max(entries.shape))
    neighbour = place[:widest] + [(place[widest] + 1) % entries.shape[widest]] + place[widest + 1:]
    return entries.at[tuple(place)].set(least).at[tuple(neighbour)].set(top_value)


def setup_inputs(seed: int = 0) -> dict:
    splits = jax.random.split(jax.random.key(seed), 3)
    populations = draw_populations(jax.random.fold_in(splits[2], 71), 0)
    fluid_mask = plant((jax.random.randint(splits[1], (NX, NZ, NY), 0, 5) < 4).astype(jnp.int32), jax.random.fold_in(splits[1], 1), 0, 1)
    return dict(populations=populations, fluid_mask=fluid_mask)


VELOCITIES = ((0, 0, 0), (1, 0, 0), (-1, 0, 0), (0, 1, 0), (0, -1, 0), (0, 0, 1), (0, 0, -1), (1, 1, 0), (-1, -1, 0), (1, -1, 0), (-1, 1, 0), (1, 0, 1), (-1, 0, -1), (1, 0, -1), (-1, 0, 1), (0, 1, 1), (0, -1, -1), (0, 1, -1), (0, -1, 1))
LATTICE_WEIGHTS = (1.0 / 3.0,) + (1.0 / 18.0,) * 6 + (1.0 / 36.0,) * 12
OPPOSITES = (0, 2, 1, 4, 3, 6, 5, 8, 7, 10, 9, 12, 11, 14, 13, 16, 15, 18, 17)
RELAX_TIME = 0.6
BODY_FORCE = 0.0001
SPEED_UNIT = 0.05

def component(which, float_type):
    return jnp.asarray([velocity[which] for velocity in VELOCITIES], float_type).reshape(19, 1, 1, 1)

def collide(current, fluid_cells):
    float_type = current.dtype
    along_x = component(0, float_type)
    along_y = component(1, float_type)
    along_z = component(2, float_type)
    weights = jnp.asarray(LATTICE_WEIGHTS, float_type).reshape(19, 1, 1, 1)
    density = lax.optimization_barrier(jnp.sum(current, axis=0))
    speed_x = lax.optimization_barrier(jnp.sum(along_x * current, axis=0)) / density
    speed_y = lax.optimization_barrier(jnp.sum(along_y * current, axis=0)) / density
    speed_z = lax.optimization_barrier(jnp.sum(along_z * current, axis=0)) / density
    project = along_x * speed_x + along_y * speed_y + along_z * speed_z
    square = speed_x * speed_x + speed_y * speed_y + speed_z * speed_z
    balance = weights * density * (1.0 + 3.0 * project + 4.5 * project * project - 1.5 * square)
    relaxed = current - (current - balance) / RELAX_TIME + 3.0 * BODY_FORCE * weights * along_x * density
    return jnp.where(fluid_cells > 0, relaxed, current)

def stream(padded):
    extent_x = padded.shape[1] - 2
    extent_z = padded.shape[2] - 2
    height = padded.shape[3]
    walled = jnp.pad(padded, ((0, 0), (0, 0), (0, 0), (1, 1)))
    fluid_self = padded[19, 1:1 + extent_x, 1:1 + extent_z, :]
    results = []
    for number in range(19):
        step_x, step_y, step_z = VELOCITIES[number]
        start_x = 1 - step_x
        start_z = 1 - step_z
        start_y = 1 - step_y
        source_value = walled[number, start_x:start_x + extent_x, start_z:start_z + extent_z, start_y:start_y + height]
        source_fluid = walled[19, start_x:start_x + extent_x, start_z:start_z + extent_z, start_y:start_y + height]
        bounce = padded[OPPOSITES[number], 1:1 + extent_x, 1:1 + extent_z, :]
        own_value = padded[number, 1:1 + extent_x, 1:1 + extent_z, :]
        arrived = jnp.where(source_fluid > 0, source_value, bounce)
        results.append(jnp.where(fluid_self > 0, arrived, own_value))
    return jnp.stack(results, axis=0)

def reference(populations, fluid_mask):
    fluid_cells = fluid_mask.astype(populations.dtype)
    current = populations
    for repeat in range(2):
        relaxed = collide(current, fluid_cells)
        stacked = jnp.concatenate([relaxed, fluid_cells[None]], axis=0)
        padded = jnp.pad(stacked, ((0, 0), (1, 1), (1, 1), (0, 0)), mode='wrap')
        current = stream(padded)
    along_x = component(0, populations.dtype)
    density = lax.optimization_barrier(jnp.sum(current, axis=0))
    speed_x = fluid_cells * lax.optimization_barrier(jnp.sum(along_x * current, axis=0)) / density
    transformed = jnp.fft.fftn(speed_x, axes=(0, 1))
    norm_scale = 1.0 / (math.sqrt(NX * NZ) * SPEED_UNIT)
    stacked_parts = jnp.stack([jnp.real(transformed), jnp.imag(transformed)], axis=0) * norm_scale
    return jnp.transpose(stacked_parts, (0, 3, 1, 2)).astype(populations.dtype)
```

```python
import math

import jax
import jax.numpy as jnp
import ml_dtypes
import numpy as np
from jax import lax
from jax.experimental import pallas as pl
from jax.experimental.pallas import tpu as pltpu
from jax.sharding import PartitionSpec as P

VELOCITIES = (
    (0, 0, 0),
    (1, 0, 0),
    (-1, 0, 0),
    (0, 1, 0),
    (0, -1, 0),
    (0, 0, 1),
    (0, 0, -1),
    (1, 1, 0),
    (-1, -1, 0),
    (1, -1, 0),
    (-1, 1, 0),
    (1, 0, 1),
    (-1, 0, -1),
    (1, 0, -1),
    (-1, 0, 1),
    (0, 1, 1),
    (0, -1, -1),
    (0, 1, -1),
    (0, -1, 1),
)
WEIGHTS = (1.0 / 3.0,) + (1.0 / 18.0,) * 6 + (1.0 / 36.0,) * 12
OPPOSITES = (0, 2, 1, 4, 3, 6, 5, 8, 7, 10, 9, 12, 11, 14, 13, 16, 15, 18, 17)
OMEGA = 1.0 / 0.6
BODY_FORCE = 0.0001
SPEED_UNIT = 0.05

DEVICES_X = 32
DEVICES_Z = 32
LAYERS = 4
COLUMNS = 16
HEIGHT = 128
NX = 128
NZ = 512
MASK = 19
RING = 24

X_UP = tuple(i for i in range(19) if VELOCITIES[i][0] == 1)
X_DOWN = tuple(i for i in range(19) if VELOCITIES[i][0] == -1)
Z_UP = tuple(i for i in range(19) if VELOCITIES[i][2] == 1)
Z_DOWN = tuple(i for i in range(19) if VELOCITIES[i][2] == -1)
Z_UNITS_UP = tuple((i, 0) for i in range(20)) + tuple((i, 1) for i in Z_UP + (MASK,))
Z_UNITS_DOWN = tuple((i, 0) for i in range(20)) + tuple((i, 1) for i in Z_DOWN + (MASK,))
Z_ROWS = len(Z_UNITS_UP) * LAYERS
X_ROWS = 6 * RING

PARAMS = pltpu.CompilerParams(vmem_limit_bytes=32 * 1024 * 1024)


def relax(current, fluid):
    plus = lambda ids: sum(current[i] for i in ids[1:]) + current[ids[0]]
    right, left = plus(X_UP), plus(X_DOWN)
    rho = plus(tuple(i for i in range(19) if VELOCITIES[i][0] == 0)) + right + left
    flow_x = right - left
    flow_y = plus(tuple(i for i in range(19) if VELOCITIES[i][1] == 1)) - plus(
        tuple(i for i in range(19) if VELOCITIES[i][1] == -1)
    )
    flow_z = plus(Z_UP) - plus(Z_DOWN)
    inverse = 1.0 / rho
    ux, uy, uz = flow_x * inverse, flow_y * inverse, flow_z * inverse
    scaled = rho * OMEGA
    rest = scaled * (1.0 - 1.5 * (ux * ux + uy * uy + uz * uz))
    odd_scale = 3.0 * scaled
    even_scale = 4.5 * scaled
    push = (3.0 * BODY_FORCE) * rho
    out = [None] * 19
    keep = 1.0 - OMEGA
    out[0] = jnp.where(fluid, keep * current[0] + WEIGHTS[0] * rest, current[0])
    for i in range(1, 19, 2):
        cx, cy, cz = VELOCITIES[i]
        parts = [u if c == 1 else -u for c, u in ((cx, ux), (cy, uy), (cz, uz)) if c]
        along = parts[0] if len(parts) == 1 else parts[0] + parts[1]
        even = WEIGHTS[i] * (rest + even_scale * (along * along))
        odd = odd_scale * along
        if cx:
            odd = odd + push if cx == 1 else odd - push
        odd = WEIGHTS[i] * odd
        j = OPPOSITES[i]
        out[i] = jnp.where(fluid, keep * current[i] + (even + odd), current[i])
        out[j] = jnp.where(fluid, keep * current[j] + (even - odd), current[j])
    return out


def collide_kernel(pop, mask, relaxed, up, down):
    for x in range(LAYERS):
        fluid_here = mask[x].astype(jnp.float32)
        out = relax([pop[i, x] for i in range(19)], fluid_here > 0)
        for i in range(19):
            relaxed[i, x] = out[i]
        for send, units, edge, step in (
            (up, Z_UNITS_UP, COLUMNS - 1, -1),
            (down, Z_UNITS_DOWN, 0, 1),
        ):
            for u, (i, depth) in enumerate(units):
                z = edge + step * depth
                value = fluid_here if i == MASK else out[i]
                send[u * LAYERS + x : u * LAYERS + x + 1, :] = value[z : z + 1, :]


def ring_tile(i, x, below, above, row):
    one = lambda ref, u: jnp.broadcast_to(ref[u * LAYERS + x : u * LAYERS + x + 1, :], (8, HEIGHT))
    tile = jnp.where(row < 4, one(above, i), one(below, i))
    if (i, 1) in Z_UNITS_DOWN:
        tile = jnp.where(row == 1, one(above, Z_UNITS_DOWN.index((i, 1))), tile)
    if (i, 1) in Z_UNITS_UP:
        tile = jnp.where(row == 6, one(below, Z_UNITS_UP.index((i, 1))), tile)
    return tile


def face_kernel(relaxed, mask, below, above, right, left):
    row = lax.broadcasted_iota(jnp.int32, (8, HEIGHT), 0)
    for send, ids, x in ((right, X_UP, LAYERS - 1), (left, X_DOWN, 0)):
        for v, i in enumerate(ids + (MASK,)):
            own = mask[x].astype(jnp.float32) if i == MASK else relaxed[i, x]
            send[v * RING : v * RING + COLUMNS, :] = own
            send[v * RING + COLUMNS : (v + 1) * RING, :] = ring_tile(i, x, below, above, row)


def step_kernel(relaxed, mask, below, above, from_left, from_right, out, first, second, planes):
    row = lax.broadcasted_iota(jnp.int32, (8, HEIGHT), 0)
    lane = lax.broadcasted_iota(jnp.int32, (RING, HEIGHT), 1)
    for i in range(20):
        for x in range(LAYERS):
            own = mask[x].astype(jnp.float32) if i == MASK else relaxed[i, x]
            first[i, x, 0:COLUMNS] = own
            first[i, x, COLUMNS:RING] = ring_tile(i, x, below, above, row)

    def moved(value, cy, cz):
        if cz:
            value = pltpu.roll(value, cz % RING, 0)
        if cy:
            value = pltpu.roll(value, cy % HEIGHT, 1)
        return value

    def fluid_moved(value, cy, cz):
        value = moved(value, cy, cz)
        if cy:
            value = jnp.where(lane == (0 if cy == 1 else HEIGHT - 1), 0.0, value)
        return value > 0

    def face(ref, ids, i):
        v = 5 if i == MASK else ids.index(i)
        return ref[v * RING : (v + 1) * RING, :]

    def fluid_at(x):
        if x < 0:
            return face(from_left, X_UP, MASK)
        if x >= LAYERS:
            return face(from_right, X_DOWN, MASK)
        return first[MASK, x]

    def source(i, x):
        if x < 0:
            return face(from_left, X_UP, i)
        if x >= LAYERS:
            return face(from_right, X_DOWN, i)
        return first[i, x]

    for x in range(LAYERS):
        fluid = fluid_at(x) > 0
        arrived = []
        for i in range(19):
            cx, cy, cz = VELOCITIES[i]
            own = first[i, x]
            if i == 0:
                arrived.append(own)
                continue
            open_path = fluid_moved(fluid_at(x - cx), cy, cz)
            value = jnp.where(open_path, moved(source(i, x - cx), cy, cz), first[OPPOSITES[i], x])
            arrived.append(jnp.where(fluid, value, own))
        for i, value in enumerate(relax(arrived, fluid)):
            second[i, x] = value

    zero = jnp.zeros((RING, HEIGHT), jnp.float32)
    for x in range(LAYERS):
        fluid = fluid_at(x) > 0
        groups = {-1: zero, 0: second[0, x], 1: zero}
        for i in range(1, 19):
            cx, cy, cz = VELOCITIES[i]
            open_path = fluid_moved(fluid_at(x - cx), cy, cz)
            inside = 0 <= x - cx < LAYERS
            value = moved(second[i, x - cx], cy, cz) if inside else zero
            groups[cx] = groups[cx] + jnp.where(open_path, value, second[OPPOSITES[i], x])
        number = jnp.where(fluid, groups[1] - groups[-1], 0.0)
        density = jnp.where(fluid, groups[0] + groups[1] + groups[-1], 1.0)
        planes[x * COLUMNS : (x + 1) * COLUMNS, :] = number[0:COLUMNS]
        planes[64 + x * COLUMNS : 64 + (x + 1) * COLUMNS, :] = density[0:COLUMNS]
    transposed = jnp.transpose(planes[...]).reshape(16, 8, HEIGHT)

    for slot, ids, x, target in ((0, X_DOWN, 0, -1), (1, X_UP, LAYERS - 1, LAYERS)):
        total = zero
        for i in ids:
            _, cy, cz = VELOCITIES[i]
            open_path = fluid_moved(fluid_at(x), cy, cz)
            total = total + jnp.where(open_path, moved(second[i, x], cy, cz), 0.0)
        total = jnp.where(fluid_at(target) > 0, total, 0.0)
        planes[slot * COLUMNS : (slot + 1) * COLUMNS, :] = total[0:COLUMNS]
    edges = jnp.transpose(planes[...]).reshape(16, 8, HEIGHT)
    for k in range(16):
        a, b = transposed[k], edges[k]
        out[16 * k : 16 * k + 8, :] = jnp.where(row < 4, a, pltpu.roll(b, 4, 0))
        out[16 * k + 8 : 16 * k + 16, :] = jnp.where(row < 4, pltpu.roll(a, 4, 0), b)


def split(value):
    high = value.astype(jnp.bfloat16)
    return high, (value - high.astype(jnp.float32)).astype(jnp.bfloat16)


def dot(a, b):
    return jnp.dot(a, b, preferred_element_type=jnp.float32)


def product(a, b):
    (a_high, a_low), (b_high, b_low) = a, b
    return dot(a_high, b_high) + (dot(a_high, b_low) + dot(a_low, b_high))


def along_x_kernel(got, high, low, out):
    lane = lax.broadcasted_iota(jnp.int32, (DEVICES_X, HEIGHT), 1)
    speeds = []
    for y in range(4):
        own = got[pl.ds(y, DEVICES_X, stride=8), :]
        edge = got[pl.ds(4 + y, DEVICES_X, stride=8), :]
        from_left = pltpu.roll(edge, 1, 0)
        from_right = pltpu.roll(edge, DEVICES_X - 1, 0)
        total = own + jnp.where(lane < 16, pltpu.roll(from_left, 112, 1), 0.0)
        total = total + jnp.where((lane >= 64) & (lane < 80), pltpu.roll(from_left, 48, 1), 0.0)
        total = total - jnp.where((lane >= 48) & (lane < 64), pltpu.roll(from_right, 48, 1), 0.0)
        total = total + jnp.where(lane >= 112, pltpu.roll(from_right, 112, 1), 0.0)
        density = jnp.where(lane < 64, pltpu.roll(total, 64, 1), 1.0)
        speeds.append(total / density)
    blocks = []
    for shift in (0, 64):
        for x in range(4):
            block = jnp.zeros((DEVICES_X, HEIGHT), jnp.float32)
            for y in range(4):
                start = shift + 16 * y
                piece = pltpu.roll(speeds[y], (start - 16 * x) % HEIGHT, 1)
                block = jnp.where((lane >= start) & (lane < start + 16), piece, block)
            blocks.append(block)
    lines = jnp.concatenate(blocks, axis=0)
    result = product((high[...], low[...]), split(lines))
    for r in range(4):
        out[pl.ds(r, DEVICES_Z, stride=4), :] = result[32 * r : 32 * r + 32, :]


def along_z_kernel(got, one_high, one_low, twist_cos, twist_sin, two_high, two_low, out):
    rows = [got[pl.ds(r, DEVICES_Z, stride=4), :] for r in range(4)]
    lines = jnp.concatenate(
        [
            jnp.concatenate([rows[0], rows[1]], axis=1),
            jnp.concatenate([rows[2], rows[3]], axis=1),
        ],
        axis=0,
    )
    inner = product((one_high[...], one_low[...]), split(lines))
    real, imag = inner[0:32], inner[32:64]
    cosine, sine = twist_cos[...], twist_sin[...]
    turned = jnp.concatenate([real * cosine + imag * sine, imag * cosine - real * sine], axis=0)
    both = product(split(turned), (two_high[...], two_low[...]))
    outer_real = both[0:32, 0:256] + both[32:64, 256:512]
    outer_imag = both[32:64, 0:256] - both[0:32, 256:512]
    for c, value in enumerate((outer_real, outer_imag)):
        columns = jnp.transpose(value)
        wide = columns.reshape(16, 16, 32)
        for quad in range(4):
            parts = [wide[:, 4 * quad + k, :] for k in range(4)]
            tile = jnp.concatenate(parts, axis=1)
            for y in range(4):
                out[c, y, :, 128 * quad : 128 * quad + 128] = tile[4 * y : 4 * y + 4]


def halves(table):
    table = np.asarray(table, np.float32)
    high = table.astype(ml_dtypes.bfloat16)
    low = (table - high.astype(np.float32)).astype(ml_dtypes.bfloat16)
    return high, low


def x_table():
    part, pair, block = np.meshgrid(np.arange(2), np.arange(2), np.arange(32), indexing="ij")
    odd, inner, outer = np.meshgrid(np.arange(2), np.arange(4), np.arange(32), indexing="ij")
    kx = (4 * block + 2 * pair).reshape(-1, 1) + odd.reshape(1, -1)
    x = (4 * outer + inner).reshape(1, -1)
    angle = 2.0 * np.pi * ((kx * x) % NX) / NX
    scale = 1.0 / (math.sqrt(NX * NZ) * SPEED_UNIT)
    return halves(np.where(part.reshape(-1, 1) == 0, np.cos(angle), -np.sin(angle)) * scale)


def z_tables():
    k, b = np.meshgrid(np.arange(32), np.arange(32), indexing="ij")
    angle = 2.0 * np.pi * ((k * b) % 32) / 32
    one = np.block([[np.cos(angle), np.sin(angle)], [-np.sin(angle), np.cos(angle)]])
    angle = 2.0 * np.pi * (np.arange(32)[:, None] * (np.arange(256) % 16)[None, :]) / NZ
    pair, odd, y, z = (v.reshape(-1, 1) for v in np.unravel_index(np.arange(256), (2, 2, 4, 16)))
    y_out, kx_out, k_out = (v.reshape(1, -1) for v in np.unravel_index(np.arange(256), (4, 4, 16)))
    same = (y == y_out) & (2 * pair + odd == kx_out)
    turn = 2.0 * np.pi * ((z * k_out) % 16) / 16
    two = np.concatenate([same * np.cos(turn), same * np.sin(turn)], axis=1)
    return (
        halves(one) + (np.cos(angle).astype(np.float32), np.sin(angle).astype(np.float32)) + halves(two)
    )


def call(kernel, name, *shapes, scratch=()):
    outs = tuple(jax.ShapeDtypeStruct(shape, jnp.float32) for shape in shapes)
    return pl.pallas_call(
        kernel,
        out_shape=outs if len(outs) > 1 else outs[0],
        scratch_shapes=[pltpu.VMEM(shape, jnp.float32) for shape in scratch],
        compiler_params=PARAMS,
        name=name,
    )


def ring(count, step):
    return [(i, (i + step) % count) for i in range(count)]


def shards(populations, fluid_mask):
    relaxed, up, down = call(
        collide_kernel,
        "collide",
        (19, LAYERS, COLUMNS, HEIGHT),
        (Z_ROWS, HEIGHT),
        (Z_ROWS, HEIGHT),
    )(populations, fluid_mask)
    below = lax.ppermute(up, "gz", ring(DEVICES_Z, 1))
    above = lax.ppermute(down, "gz", ring(DEVICES_Z, -1))
    right, left = call(face_kernel, "faces", (X_ROWS, HEIGHT), (X_ROWS, HEIGHT))(
        relaxed, fluid_mask, below, above
    )
    from_left = lax.ppermute(right, "gx", ring(DEVICES_X, 1))
    from_right = lax.ppermute(left, "gx", ring(DEVICES_X, -1))
    sums = call(
        step_kernel,
        "steps",
        (8 * DEVICES_X, HEIGHT),
        scratch=((20, LAYERS, RING, HEIGHT), (19, LAYERS, RING, HEIGHT), (HEIGHT, HEIGHT)),
    )(relaxed, fluid_mask, below, above, from_left, from_right)
    lines = lax.all_to_all(sums, "gx", split_axis=0, concat_axis=0, tiled=True)
    spectrum = call(along_x_kernel, "along_x", (4 * DEVICES_Z, HEIGHT))(lines, *x_table())
    spectrum = lax.all_to_all(spectrum, "gz", split_axis=0, concat_axis=0, tiled=True)
    return call(along_z_kernel, "along_z", (2, 4, 4, NZ))(spectrum, *z_tables())


def solution(mesh):
    placed = (P(None, "gx", "gz", None), P("gx", "gz", None))
    return jax.shard_map(
        shards, mesh=mesh, in_specs=placed, out_specs=P(None, "gx", "gz", None), check_vma=False
    )
```

```python
import math

import jax
import jax.numpy as jnp
import ml_dtypes
import numpy as np
from jax import lax
from jax.experimental import pallas as pl
from jax.experimental.pallas import tpu as pltpu
from jax.sharding import PartitionSpec as P

VELOCITIES = (
    (0, 0, 0),
    (1, 0, 0),
    (-1, 0, 0),
    (0, 1, 0),
    (0, -1, 0),
    (0, 0, 1),
    (0, 0, -1),
    (1, 1, 0),
    (-1, -1, 0),
    (1, -1, 0),
    (-1, 1, 0),
    (1, 0, 1),
    (-1, 0, -1),
    (1, 0, -1),
    (-1, 0, 1),
    (0, 1, 1),
    (0, -1, -1),
    (0, 1, -1),
    (0, -1, 1),
)
WEIGHTS = (1.0 / 3.0,) + (1.0 / 18.0,) * 6 + (1.0 / 36.0,) * 12
OPPOSITES = (0, 2, 1, 4, 3, 6, 5, 8, 7, 10, 9, 12, 11, 14, 13, 16, 15, 18, 17)
OMEGA = 1.0 / 0.6
BODY_FORCE = 0.0001
SPEED_UNIT = 0.05

DEVICES_X = 32
DEVICES_Z = 32
LAYERS = 4
COLUMNS = 16
HEIGHT = 128
NX = 128
NZ = 512
MASK = 19
RING = 24

X_UP = tuple(i for i in range(19) if VELOCITIES[i][0] == 1)
X_DOWN = tuple(i for i in range(19) if VELOCITIES[i][0] == -1)
Z_UP = tuple(i for i in range(19) if VELOCITIES[i][2] == 1)
Z_DOWN = tuple(i for i in range(19) if VELOCITIES[i][2] == -1)
Z_UNITS_UP = tuple((i, 0) for i in range(20)) + tuple((i, 1) for i in Z_UP + (MASK,))
Z_UNITS_DOWN = tuple((i, 0) for i in range(20)) + tuple((i, 1) for i in Z_DOWN + (MASK,))
Z_ROWS = len(Z_UNITS_UP) * LAYERS
X_ROWS = 6 * RING

PARAMS = pltpu.CompilerParams(vmem_limit_bytes=32 * 1024 * 1024)


def relax(current, fluid):
    plus = lambda ids: sum(current[i] for i in ids[1:]) + current[ids[0]]
    right, left = plus(X_UP), plus(X_DOWN)
    rho = plus(tuple(i for i in range(19) if VELOCITIES[i][0] == 0)) + right + left
    flow_x = right - left
    flow_y = plus(tuple(i for i in range(19) if VELOCITIES[i][1] == 1)) - plus(
        tuple(i for i in range(19) if VELOCITIES[i][1] == -1)
    )
    flow_z = plus(Z_UP) - plus(Z_DOWN)
    inverse = 1.0 / rho
    ux, uy, uz = flow_x * inverse, flow_y * inverse, flow_z * inverse
    scaled = rho * OMEGA
    rest = scaled * (1.0 - 1.5 * (ux * ux + uy * uy + uz * uz))
    odd_scale = 3.0 * scaled
    even_scale = 4.5 * scaled
    push = (3.0 * BODY_FORCE) * rho
    out = [None] * 19
    keep = 1.0 - OMEGA
    out[0] = jnp.where(fluid, keep * current[0] + WEIGHTS[0] * rest, current[0])
    for i in range(1, 19, 2):
        cx, cy, cz = VELOCITIES[i]
        parts = [u if c == 1 else -u for c, u in ((cx, ux), (cy, uy), (cz, uz)) if c]
        along = parts[0] if len(parts) == 1 else parts[0] + parts[1]
        even = WEIGHTS[i] * (rest + even_scale * (along * along))
        odd = odd_scale * along
        if cx:
            odd = odd + push if cx == 1 else odd - push
        odd = WEIGHTS[i] * odd
        j = OPPOSITES[i]
        out[i] = jnp.where(fluid, keep * current[i] + (even + odd), current[i])
        out[j] = jnp.where(fluid, keep * current[j] + (even - odd), current[j])
    return out


def even_index(axis):
    return lax.axis_index(axis) % 2 == 0


def collide_kernel(pop, mask, relaxed, far, near, held, solid, up, down, arrivals):
    copies = [
        pltpu.make_async_copy(pop.at[:, x], held.at[:, x], arrivals.at[x]) for x in range(LAYERS)
    ]
    copies.append(pltpu.make_async_copy(mask, solid, arrivals.at[LAYERS]))
    for copy in copies:
        copy.start()
    copies[LAYERS].wait()
    for x in range(LAYERS):
        copies[x].wait()
        fluid_here = solid[x].astype(jnp.float32)
        out = relax([held[i, x] for i in range(19)], fluid_here > 0) + [fluid_here]
        for i in range(20):
            relaxed[i, x] = out[i]
        for send, units, edge, step in (
            (up, Z_UNITS_UP, COLUMNS - 1, -1),
            (down, Z_UNITS_DOWN, 0, 1),
        ):
            for u, (i, depth) in enumerate(units):
                z = edge + step * depth
                send[u * LAYERS + x : u * LAYERS + x + 1, :] = out[i][z : z + 1, :]
    even = even_index("gz")
    near[...] = jnp.where(even, up[...], down[...])
    far[...] = jnp.where(even, down[...], up[...])


def ring_tile(i, x, below, above, row):
    one = lambda ref, u: jnp.broadcast_to(ref[u * LAYERS + x : u * LAYERS + x + 1, :], (8, HEIGHT))
    tile = jnp.where(row < 4, one(above, i), one(below, i))
    if (i, 1) in Z_UNITS_DOWN:
        tile = jnp.where(row == 1, one(above, Z_UNITS_DOWN.index((i, 1))), tile)
    if (i, 1) in Z_UNITS_UP:
        tile = jnp.where(row == 6, one(below, Z_UNITS_UP.index((i, 1))), tile)
    return tile


def face_kernel(relaxed, z_far, z_near, far, near, below, above, right, left):
    even = even_index("gz")
    below[...] = jnp.where(even, z_far[...], z_near[...])
    above[...] = jnp.where(even, z_near[...], z_far[...])
    row = lax.broadcasted_iota(jnp.int32, (8, HEIGHT), 0)
    for send, ids, x in ((right, X_UP, LAYERS - 1), (left, X_DOWN, 0)):
        for v, i in enumerate(ids + (MASK,)):
            send[v * RING : v * RING + COLUMNS, :] = relaxed[i, x]
            send[v * RING + COLUMNS : (v + 1) * RING, :] = ring_tile(i, x, below, above, row)
    even = even_index("gx")
    near[...] = jnp.where(even, right[...], left[...])
    far[...] = jnp.where(even, left[...], right[...])


def step_kernel(
    relaxed, z_far, z_near, x_far, x_near, out, first, second, planes, below, above, from_left, from_right
):
    even = even_index("gz")
    below[...] = jnp.where(even, z_far[...], z_near[...])
    above[...] = jnp.where(even, z_near[...], z_far[...])
    even = even_index("gx")
    from_left[...] = jnp.where(even, x_far[...], x_near[...])
    from_right[...] = jnp.where(even, x_near[...], x_far[...])
    row = lax.broadcasted_iota(jnp.int32, (8, HEIGHT), 0)
    lane = lax.broadcasted_iota(jnp.int32, (RING, HEIGHT), 1)
    for i in range(20):
        for x in range(LAYERS):
            first[i, x, 0:COLUMNS] = relaxed[i, x]
            first[i, x, COLUMNS:RING] = ring_tile(i, x, below, above, row)

    def moved(value, cy, cz):
        if cz:
            value = pltpu.roll(value, cz % RING, 0)
        if cy:
            value = pltpu.roll(value, cy % HEIGHT, 1)
        return value

    def fluid_moved(value, cy, cz):
        value = moved(value, cy, cz)
        if cy:
            value = jnp.where(lane == (0 if cy == 1 else HEIGHT - 1), 0.0, value)
        return value > 0

    def face(ref, ids, i):
        v = 5 if i == MASK else ids.index(i)
        return ref[v * RING : (v + 1) * RING, :]

    def fluid_at(x):
        if x < 0:
            return face(from_left, X_UP, MASK)
        if x >= LAYERS:
            return face(from_right, X_DOWN, MASK)
        return first[MASK, x]

    def source(i, x):
        if x < 0:
            return face(from_left, X_UP, i)
        if x >= LAYERS:
            return face(from_right, X_DOWN, i)
        return first[i, x]

    for x in range(LAYERS):
        fluid = fluid_at(x) > 0
        arrived = []
        for i in range(19):
            cx, cy, cz = VELOCITIES[i]
            own = first[i, x]
            if i == 0:
                arrived.append(own)
                continue
            open_path = fluid_moved(fluid_at(x - cx), cy, cz)
            value = jnp.where(open_path, moved(source(i, x - cx), cy, cz), first[OPPOSITES[i], x])
            arrived.append(jnp.where(fluid, value, own))
        for i, value in enumerate(relax(arrived, fluid)):
            second[i, x] = value

    zero = jnp.zeros((RING, HEIGHT), jnp.float32)
    for x in range(LAYERS):
        fluid = fluid_at(x) > 0
        groups = {-1: zero, 0: second[0, x], 1: zero}
        for i in range(1, 19):
            cx, cy, cz = VELOCITIES[i]
            open_path = fluid_moved(fluid_at(x - cx), cy, cz)
            inside = 0 <= x - cx < LAYERS
            value = moved(second[i, x - cx], cy, cz) if inside else zero
            groups[cx] = groups[cx] + jnp.where(open_path, value, second[OPPOSITES[i], x])
        number = jnp.where(fluid, groups[1] - groups[-1], 0.0)
        density = jnp.where(fluid, groups[0] + groups[1] + groups[-1], 1.0)
        planes[x * COLUMNS : (x + 1) * COLUMNS, :] = number[0:COLUMNS]
        planes[64 + x * COLUMNS : 64 + (x + 1) * COLUMNS, :] = density[0:COLUMNS]
    transposed = jnp.transpose(planes[...]).reshape(16, 8, HEIGHT)

    for slot, ids, x, target in ((0, X_DOWN, 0, -1), (1, X_UP, LAYERS - 1, LAYERS)):
        total = zero
        for i in ids:
            _, cy, cz = VELOCITIES[i]
            open_path = fluid_moved(fluid_at(x), cy, cz)
            total = total + jnp.where(open_path, moved(second[i, x], cy, cz), 0.0)
        total = jnp.where(fluid_at(target) > 0, total, 0.0)
        planes[slot * COLUMNS : (slot + 1) * COLUMNS, :] = total[0:COLUMNS]
    edges = jnp.transpose(planes[...]).reshape(16, 8, HEIGHT)
    for k in range(16):
        a, b = transposed[k], edges[k]
        out[16 * k : 16 * k + 8, :] = jnp.where(row < 4, a, pltpu.roll(b, 4, 0))
        out[16 * k + 8 : 16 * k + 16, :] = jnp.where(row < 4, pltpu.roll(a, 4, 0), b)


def split(value):
    high = value.astype(jnp.bfloat16)
    return high, (value - high.astype(jnp.float32)).astype(jnp.bfloat16)


def dot(a, b):
    return jnp.dot(a, b, preferred_element_type=jnp.float32)


def product(a, b):
    (a_high, a_low), (b_high, b_low) = a, b
    return dot(a_high, b_high) + (dot(a_high, b_low) + dot(a_low, b_high))


def along_x_kernel(got, high, low, out):
    lane = lax.broadcasted_iota(jnp.int32, (DEVICES_X, HEIGHT), 1)
    speeds = []
    for y in range(4):
        own = got[pl.ds(y, DEVICES_X, stride=8), :]
        edge = got[pl.ds(4 + y, DEVICES_X, stride=8), :]
        from_left = pltpu.roll(edge, 1, 0)
        from_right = pltpu.roll(edge, DEVICES_X - 1, 0)
        total = own + jnp.where(lane < 16, pltpu.roll(from_left, 112, 1), 0.0)
        total = total + jnp.where((lane >= 64) & (lane < 80), pltpu.roll(from_left, 48, 1), 0.0)
        total = total - jnp.where((lane >= 48) & (lane < 64), pltpu.roll(from_right, 48, 1), 0.0)
        total = total + jnp.where(lane >= 112, pltpu.roll(from_right, 112, 1), 0.0)
        density = jnp.where(lane < 64, pltpu.roll(total, 64, 1), 1.0)
        speeds.append(total / density)
    blocks = []
    for shift in (0, 64):
        for x in range(4):
            block = jnp.zeros((DEVICES_X, HEIGHT), jnp.float32)
            for y in range(4):
                start = shift + 16 * y
                piece = pltpu.roll(speeds[y], (start - 16 * x) % HEIGHT, 1)
                block = jnp.where((lane >= start) & (lane < start + 16), piece, block)
            blocks.append(block)
    lines = jnp.concatenate(blocks, axis=0)
    result = product((high[...], low[...]), split(lines))
    for r in range(4):
        out[pl.ds(r, DEVICES_Z, stride=4), :] = result[32 * r : 32 * r + 32, :]


def along_z_kernel(got, one_high, one_low, twist_cos, twist_sin, two_high, two_low, out):
    rows = [got[pl.ds(r, DEVICES_Z, stride=4), :] for r in range(4)]
    lines = jnp.concatenate(
        [
            jnp.concatenate([rows[0], rows[1]], axis=1),
            jnp.concatenate([rows[2], rows[3]], axis=1),
        ],
        axis=0,
    )
    inner = product((one_high[...], one_low[...]), split(lines))
    real, imag = inner[0:32], inner[32:64]
    cosine, sine = twist_cos[...], twist_sin[...]
    turned = jnp.concatenate([real * cosine + imag * sine, imag * cosine - real * sine], axis=0)
    both = product(split(turned), (two_high[...], two_low[...]))
    outer_real = both[0:32, 0:256] + both[32:64, 256:512]
    outer_imag = both[32:64, 0:256] - both[0:32, 256:512]
    for c, value in enumerate((outer_real, outer_imag)):
        columns = jnp.transpose(value)
        wide = columns.reshape(16, 16, 32)
        for quad in range(4):
            parts = [wide[:, 4 * quad + k, :] for k in range(4)]
            tile = jnp.concatenate(parts, axis=1)
            for y in range(4):
                out[c, y, :, 128 * quad : 128 * quad + 128] = tile[4 * y : 4 * y + 4]


def halves(table):
    table = np.asarray(table, np.float32)
    high = table.astype(ml_dtypes.bfloat16)
    low = (table - high.astype(np.float32)).astype(ml_dtypes.bfloat16)
    return high, low


def x_table():
    part, pair, block = np.meshgrid(np.arange(2), np.arange(2), np.arange(32), indexing="ij")
    odd, inner, outer = np.meshgrid(np.arange(2), np.arange(4), np.arange(32), indexing="ij")
    kx = (4 * block + 2 * pair).reshape(-1, 1) + odd.reshape(1, -1)
    x = (4 * outer + inner).reshape(1, -1)
    angle = 2.0 * np.pi * ((kx * x) % NX) / NX
    scale = 1.0 / (math.sqrt(NX * NZ) * SPEED_UNIT)
    return halves(np.where(part.reshape(-1, 1) == 0, np.cos(angle), -np.sin(angle)) * scale)


def z_tables():
    k, b = np.meshgrid(np.arange(32), np.arange(32), indexing="ij")
    angle = 2.0 * np.pi * ((k * b) % 32) / 32
    one = np.block([[np.cos(angle), np.sin(angle)], [-np.sin(angle), np.cos(angle)]])
    angle = 2.0 * np.pi * (np.arange(32)[:, None] * (np.arange(256) % 16)[None, :]) / NZ
    pair, odd, y, z = (v.reshape(-1, 1) for v in np.unravel_index(np.arange(256), (2, 2, 4, 16)))
    y_out, kx_out, k_out = (v.reshape(1, -1) for v in np.unravel_index(np.arange(256), (4, 4, 16)))
    same = (y == y_out) & (2 * pair + odd == kx_out)
    turn = 2.0 * np.pi * ((z * k_out) % 16) / 16
    two = np.concatenate([same * np.cos(turn), same * np.sin(turn)], axis=1)
    return (
        halves(one) + (np.cos(angle).astype(np.float32), np.sin(angle).astype(np.float32)) + halves(two)
    )


def call(kernel, name, *shapes, scratch=(), in_specs=None):
    outs = tuple(jax.ShapeDtypeStruct(shape, jnp.float32) for shape in shapes)
    return pl.pallas_call(
        kernel,
        out_shape=outs if len(outs) > 1 else outs[0],
        **({} if in_specs is None else {"in_specs": in_specs}),
        scratch_shapes=[
            pltpu.VMEM(shape, jnp.float32) if isinstance(shape, tuple) else shape
            for shape in scratch
        ],
        compiler_params=PARAMS,
        name=name,
    )


def near_pairs(count):
    return [(i, i ^ 1) for i in range(count)]


def far_pairs(count):
    return [(i, (i + (1 if i % 2 else -1)) % count) for i in range(count)]


def swap(near, far, axis, count):
    near = lax.ppermute(near, axis, near_pairs(count))
    far = lax.ppermute(far, axis, far_pairs(count))
    return near, far


def shards(populations, fluid_mask):
    block = (LAYERS, COLUMNS, HEIGHT)
    z_edge = (Z_ROWS, HEIGHT)
    x_edge = (X_ROWS, HEIGHT)
    relaxed, far, near = call(
        collide_kernel,
        "collide",
        (20,) + block,
        z_edge,
        z_edge,
        in_specs=[pl.BlockSpec(memory_space=pltpu.HBM)] * 2,
        scratch=(
            (19,) + block,
            pltpu.VMEM(block, jnp.int32),
            z_edge,
            z_edge,
            pltpu.SemaphoreType.DMA((LAYERS + 1,)),
        ),
    )(
        pltpu.with_memory_space_constraint(populations, pltpu.HBM),
        pltpu.with_memory_space_constraint(fluid_mask, pltpu.HBM),
    )
    z_near, z_far = swap(near, far, "gz", DEVICES_Z)
    far, near = call(face_kernel, "faces", x_edge, x_edge, scratch=(z_edge, z_edge, x_edge, x_edge))(
        relaxed, z_far, z_near
    )
    x_near, x_far = swap(near, far, "gx", DEVICES_X)
    sums = call(
        step_kernel,
        "steps",
        (8 * DEVICES_X, HEIGHT),
        scratch=(
            (20, LAYERS, RING, HEIGHT),
            (19, LAYERS, RING, HEIGHT),
            (HEIGHT, HEIGHT),
            z_edge,
            z_edge,
            x_edge,
            x_edge,
        ),
    )(relaxed, z_far, z_near, x_far, x_near)
    lines = lax.all_to_all(sums, "gx", split_axis=0, concat_axis=0, tiled=True)
    spectrum = call(along_x_kernel, "along_x", (4 * DEVICES_Z, HEIGHT))(lines, *x_table())
    spectrum = lax.all_to_all(spectrum, "gz", split_axis=0, concat_axis=0, tiled=True)
    return call(along_z_kernel, "along_z", (2, 4, 4, NZ))(spectrum, *z_tables())


def solution(mesh):
    placed = (P(None, "gx", "gz", None), P("gx", "gz", None))
    return jax.shard_map(
        shards, mesh=mesh, in_specs=placed, out_specs=P(None, "gx", "gz", None), check_vma=False
    )
```

```python
import math

import jax
import jax.numpy as jnp
import ml_dtypes
import numpy as np
from jax import lax
from jax.experimental import pallas as pl
from jax.experimental.pallas import tpu as pltpu
from jax.sharding import PartitionSpec as P

VELOCITIES = (
    (0, 0, 0),
    (1, 0, 0),
    (-1, 0, 0),
    (0, 1, 0),
    (0, -1, 0),
    (0, 0, 1),
    (0, 0, -1),
    (1, 1, 0),
    (-1, -1, 0),
    (1, -1, 0),
    (-1, 1, 0),
    (1, 0, 1),
    (-1, 0, -1),
    (1, 0, -1),
    (-1, 0, 1),
    (0, 1, 1),
    (0, -1, -1),
    (0, 1, -1),
    (0, -1, 1),
)
WEIGHTS = (1.0 / 3.0,) + (1.0 / 18.0,) * 6 + (1.0 / 36.0,) * 12
OPPOSITES = (0, 2, 1, 4, 3, 6, 5, 8, 7, 10, 9, 12, 11, 14, 13, 16, 15, 18, 17)
OMEGA = 1.0 / 0.6
BODY_FORCE = 0.0001
SPEED_UNIT = 0.05

DEVICES_X = 32
DEVICES_Z = 32
LAYERS = 4
COLUMNS = 16
HEIGHT = 128
NX = 128
NZ = 512
MASK = 19
RING = 24
FIRST_X = 18
FIRST_Z = 21

X_UP = tuple(i for i in range(19) if VELOCITIES[i][0] == 1)
X_DOWN = tuple(i for i in range(19) if VELOCITIES[i][0] == -1)
Z_UP = tuple(i for i in range(19) if VELOCITIES[i][2] == 1)
Z_DOWN = tuple(i for i in range(19) if VELOCITIES[i][2] == -1)
Z_UNITS_UP = tuple((i, 0) for i in range(20)) + tuple((i, 1) for i in Z_UP + (MASK,))
Z_UNITS_DOWN = tuple((i, 0) for i in range(20)) + tuple((i, 1) for i in Z_DOWN + (MASK,))
Z_ROWS = len(Z_UNITS_UP) * LAYERS
X_ROWS = 6 * RING

PARAMS = pltpu.CompilerParams(vmem_limit_bytes=32 * 1024 * 1024)


def relax(current, fluid):
    plus = lambda ids: sum(current[i] for i in ids[1:]) + current[ids[0]]
    right, left = plus(X_UP), plus(X_DOWN)
    rho = plus(tuple(i for i in range(19) if VELOCITIES[i][0] == 0)) + right + left
    flow_x = right - left
    flow_y = plus(tuple(i for i in range(19) if VELOCITIES[i][1] == 1)) - plus(
        tuple(i for i in range(19) if VELOCITIES[i][1] == -1)
    )
    flow_z = plus(Z_UP) - plus(Z_DOWN)
    inverse = 1.0 / rho
    ux, uy, uz = flow_x * inverse, flow_y * inverse, flow_z * inverse
    scaled = rho * OMEGA
    rest = scaled * (1.0 - 1.5 * (ux * ux + uy * uy + uz * uz))
    odd_scale = 3.0 * scaled
    even_scale = 4.5 * scaled
    push = (3.0 * BODY_FORCE) * rho
    out = [None] * 19
    keep = 1.0 - OMEGA
    out[0] = jnp.where(fluid, keep * current[0] + WEIGHTS[0] * rest, current[0])
    for i in range(1, 19, 2):
        cx, cy, cz = VELOCITIES[i]
        parts = [u if c == 1 else -u for c, u in ((cx, ux), (cy, uy), (cz, uz)) if c]
        along = parts[0] if len(parts) == 1 else parts[0] + parts[1]
        even = WEIGHTS[i] * (rest + even_scale * (along * along))
        odd = odd_scale * along
        if cx:
            odd = odd + push if cx == 1 else odd - push
        odd = WEIGHTS[i] * odd
        j = OPPOSITES[i]
        out[i] = jnp.where(fluid, keep * current[i] + (even + odd), current[i])
        out[j] = jnp.where(fluid, keep * current[j] + (even - odd), current[j])
    return out


def even_index(axis):
    return lax.axis_index(axis) % 2 == 0


def collide_kernel(pop, mask, relaxed, far, near, held, solid, up, down, arrivals):
    copies = [
        pltpu.make_async_copy(pop.at[:, x], held.at[:, x], arrivals.at[x]) for x in range(LAYERS)
    ]
    copies.append(pltpu.make_async_copy(mask, solid, arrivals.at[LAYERS]))
    for copy in copies:
        copy.start()
    copies[LAYERS].wait()
    for x in range(LAYERS):
        copies[x].wait()
        fluid_here = solid[x].astype(jnp.float32)
        out = relax([held[i, x] for i in range(19)], fluid_here > 0) + [fluid_here]
        for i in range(20):
            relaxed[i, x] = out[i]
        for send, units, edge, step in (
            (up, Z_UNITS_UP, COLUMNS - 1, -1),
            (down, Z_UNITS_DOWN, 0, 1),
        ):
            for u, (i, depth) in enumerate(units):
                z = edge + step * depth
                send[u * LAYERS + x : u * LAYERS + x + 1, :] = out[i][z : z + 1, :]
    even = even_index("gz")
    near[...] = jnp.where(even, up[...], down[...])
    far[...] = jnp.where(even, down[...], up[...])


def ring_tile(i, x, below, above, row):
    one = lambda ref, u: jnp.broadcast_to(ref[u * LAYERS + x : u * LAYERS + x + 1, :], (8, HEIGHT))
    tile = jnp.where(row < 4, one(above, i), one(below, i))
    if (i, 1) in Z_UNITS_DOWN:
        tile = jnp.where(row == 1, one(above, Z_UNITS_DOWN.index((i, 1))), tile)
    if (i, 1) in Z_UNITS_UP:
        tile = jnp.where(row == 6, one(below, Z_UNITS_UP.index((i, 1))), tile)
    return tile


def face_kernel(relaxed, z_far, z_near, far, near, below, above, right, left):
    even = even_index("gz")
    below[...] = jnp.where(even, z_far[...], z_near[...])
    above[...] = jnp.where(even, z_near[...], z_far[...])
    row = lax.broadcasted_iota(jnp.int32, (8, HEIGHT), 0)
    for send, ids, x in ((right, X_UP, LAYERS - 1), (left, X_DOWN, 0)):
        for v, i in enumerate(ids + (MASK,)):
            send[v * RING : v * RING + COLUMNS, :] = relaxed[i, x]
            send[v * RING + COLUMNS : (v + 1) * RING, :] = ring_tile(i, x, below, above, row)
    even = even_index("gx")
    near[...] = jnp.where(even, right[...], left[...])
    far[...] = jnp.where(even, left[...], right[...])


def step_kernel(
    relaxed, z_far, z_near, x_far, x_near, out, first, second, planes, below, above, from_left, from_right
):
    even = even_index("gz")
    below[...] = jnp.where(even, z_far[...], z_near[...])
    above[...] = jnp.where(even, z_near[...], z_far[...])
    even = even_index("gx")
    from_left[...] = jnp.where(even, x_far[...], x_near[...])
    from_right[...] = jnp.where(even, x_near[...], x_far[...])
    row = lax.broadcasted_iota(jnp.int32, (8, HEIGHT), 0)
    lane = lax.broadcasted_iota(jnp.int32, (RING, HEIGHT), 1)
    for i in range(20):
        for x in range(LAYERS):
            first[i, x, 0:COLUMNS] = relaxed[i, x]
            first[i, x, COLUMNS:RING] = ring_tile(i, x, below, above, row)

    def moved(value, cy, cz):
        if cz:
            value = pltpu.roll(value, cz % RING, 0)
        if cy:
            value = pltpu.roll(value, cy % HEIGHT, 1)
        return value

    def fluid_moved(value, cy, cz):
        value = moved(value, cy, cz)
        if cy:
            value = jnp.where(lane == (0 if cy == 1 else HEIGHT - 1), 0.0, value)
        return value > 0

    def face(ref, ids, i):
        v = 5 if i == MASK else ids.index(i)
        return ref[v * RING : (v + 1) * RING, :]

    def fluid_at(x):
        if x < 0:
            return face(from_left, X_UP, MASK)
        if x >= LAYERS:
            return face(from_right, X_DOWN, MASK)
        return first[MASK, x]

    def source(i, x):
        if x < 0:
            return face(from_left, X_UP, i)
        if x >= LAYERS:
            return face(from_right, X_DOWN, i)
        return first[i, x]

    for x in range(LAYERS):
        fluid = fluid_at(x) > 0
        arrived = []
        for i in range(19):
            cx, cy, cz = VELOCITIES[i]
            own = first[i, x]
            if i == 0:
                arrived.append(own)
                continue
            open_path = fluid_moved(fluid_at(x - cx), cy, cz)
            value = jnp.where(open_path, moved(source(i, x - cx), cy, cz), first[OPPOSITES[i], x])
            arrived.append(jnp.where(fluid, value, own))
        for i, value in enumerate(relax(arrived, fluid)):
            second[i, x] = value

    zero = jnp.zeros((RING, HEIGHT), jnp.float32)
    for x in range(LAYERS):
        fluid = fluid_at(x) > 0
        groups = {-1: zero, 0: second[0, x], 1: zero}
        for i in range(1, 19):
            cx, cy, cz = VELOCITIES[i]
            open_path = fluid_moved(fluid_at(x - cx), cy, cz)
            inside = 0 <= x - cx < LAYERS
            value = moved(second[i, x - cx], cy, cz) if inside else zero
            groups[cx] = groups[cx] + jnp.where(open_path, value, second[OPPOSITES[i], x])
        number = jnp.where(fluid, groups[1] - groups[-1], 0.0)
        density = jnp.where(fluid, groups[0] + groups[1] + groups[-1], 1.0)
        planes[x * COLUMNS : (x + 1) * COLUMNS, :] = number[0:COLUMNS]
        planes[64 + x * COLUMNS : 64 + (x + 1) * COLUMNS, :] = density[0:COLUMNS]
    transposed = jnp.transpose(planes[...]).reshape(16, 8, HEIGHT)

    for slot, ids, x, target in ((0, X_DOWN, 0, -1), (1, X_UP, LAYERS - 1, LAYERS)):
        total = zero
        for i in ids:
            _, cy, cz = VELOCITIES[i]
            open_path = fluid_moved(fluid_at(x), cy, cz)
            total = total + jnp.where(open_path, moved(second[i, x], cy, cz), 0.0)
        total = jnp.where(fluid_at(target) > 0, total, 0.0)
        planes[slot * COLUMNS : (slot + 1) * COLUMNS, :] = total[0:COLUMNS]
    edges = jnp.transpose(planes[...]).reshape(16, 8, HEIGHT)
    for k in range(16):
        a, b = transposed[k], edges[k]
        for device, tile in (
            (2 * k, jnp.where(row < 4, a, pltpu.roll(b, 4, 0))),
            (2 * k + 1, jnp.where(row < 4, pltpu.roll(a, 4, 0), b)),
        ):
            place = 8 * ((device - FIRST_X) % DEVICES_X)
            out[place : place + 8, :] = tile


def split(value):
    high = value.astype(jnp.bfloat16)
    return high, (value - high.astype(jnp.float32)).astype(jnp.bfloat16)


def dot(a, b):
    return jnp.dot(a, b, preferred_element_type=jnp.float32)


def product(a, b):
    (a_high, a_low), (b_high, b_low) = a, b
    return dot(a_high, b_high) + (dot(a_high, b_low) + dot(a_low, b_high))


def along_x_kernel(got, high, low, out):
    lane = lax.broadcasted_iota(jnp.int32, (DEVICES_X, HEIGHT), 1)
    speeds = []
    for y in range(4):
        own = got[pl.ds(y, DEVICES_X, stride=8), :]
        edge = got[pl.ds(4 + y, DEVICES_X, stride=8), :]
        from_left = pltpu.roll(edge, 1, 0)
        from_right = pltpu.roll(edge, DEVICES_X - 1, 0)
        total = own + jnp.where(lane < 16, pltpu.roll(from_left, 112, 1), 0.0)
        total = total + jnp.where((lane >= 64) & (lane < 80), pltpu.roll(from_left, 48, 1), 0.0)
        total = total - jnp.where((lane >= 48) & (lane < 64), pltpu.roll(from_right, 48, 1), 0.0)
        total = total + jnp.where(lane >= 112, pltpu.roll(from_right, 112, 1), 0.0)
        density = jnp.where(lane < 64, pltpu.roll(total, 64, 1), 1.0)
        speeds.append(total / density)
    blocks = []
    for shift in (0, 64):
        for x in range(4):
            block = jnp.zeros((DEVICES_X, HEIGHT), jnp.float32)
            for y in range(4):
                start = shift + 16 * y
                piece = pltpu.roll(speeds[y], (start - 16 * x) % HEIGHT, 1)
                block = jnp.where((lane >= start) & (lane < start + 16), piece, block)
            blocks.append(block)
    lines = jnp.concatenate(blocks, axis=0)
    result = product((high[...], low[...]), split(lines))
    for r in range(4):
        out[pl.ds(r, DEVICES_Z, stride=4), :] = result[32 * r : 32 * r + 32, :]


def along_z_kernel(got, one_high, one_low, twist_cos, twist_sin, two_high, two_low, out):
    rows = [got[pl.ds(r, DEVICES_Z, stride=4), :] for r in range(4)]
    lines = jnp.concatenate(
        [
            jnp.concatenate([rows[0], rows[1]], axis=1),
            jnp.concatenate([rows[2], rows[3]], axis=1),
        ],
        axis=0,
    )
    inner = product((one_high[...], one_low[...]), split(lines))
    real, imag = inner[0:32], inner[32:64]
    cosine, sine = twist_cos[...], twist_sin[...]
    turned = jnp.concatenate([real * cosine + imag * sine, imag * cosine - real * sine], axis=0)
    both = product(split(turned), (two_high[...], two_low[...]))
    outer_real = both[0:32, 0:256] + both[32:64, 256:512]
    outer_imag = both[32:64, 0:256] - both[0:32, 256:512]
    for c, value in enumerate((outer_real, outer_imag)):
        columns = jnp.transpose(value)
        wide = columns.reshape(16, 16, 32)
        for quad in range(4):
            parts = [wide[:, 4 * quad + k, :] for k in range(4)]
            tile = jnp.concatenate(parts, axis=1)
            for y in range(4):
                out[c, y, :, 128 * quad : 128 * quad + 128] = tile[4 * y : 4 * y + 4]


def halves(table):
    table = np.asarray(table, np.float32)
    high = table.astype(ml_dtypes.bfloat16)
    low = (table - high.astype(np.float32)).astype(ml_dtypes.bfloat16)
    return high, low


def x_table():
    part, pair, block = np.meshgrid(np.arange(2), np.arange(2), np.arange(32), indexing="ij")
    odd, inner, outer = np.meshgrid(np.arange(2), np.arange(4), np.arange(32), indexing="ij")
    kx = (4 * ((block + FIRST_Z) % 32) + 2 * pair).reshape(-1, 1) + odd.reshape(1, -1)
    x = (4 * ((outer + FIRST_X) % 32) + inner).reshape(1, -1)
    angle = 2.0 * np.pi * ((kx * x) % NX) / NX
    scale = 1.0 / (math.sqrt(NX * NZ) * SPEED_UNIT)
    return halves(np.where(part.reshape(-1, 1) == 0, np.cos(angle), -np.sin(angle)) * scale)


def z_tables():
    k, b = np.meshgrid(np.arange(32), (np.arange(32) + FIRST_Z) % 32, indexing="ij")
    angle = 2.0 * np.pi * ((k * b) % 32) / 32
    one = np.block([[np.cos(angle), np.sin(angle)], [-np.sin(angle), np.cos(angle)]])
    angle = 2.0 * np.pi * (np.arange(32)[:, None] * (np.arange(256) % 16)[None, :]) / NZ
    pair, odd, y, z = (v.reshape(-1, 1) for v in np.unravel_index(np.arange(256), (2, 2, 4, 16)))
    y_out, kx_out, k_out = (v.reshape(1, -1) for v in np.unravel_index(np.arange(256), (4, 4, 16)))
    same = (y == y_out) & (2 * pair + odd == kx_out)
    turn = 2.0 * np.pi * ((z * k_out) % 16) / 16
    two = np.concatenate([same * np.cos(turn), same * np.sin(turn)], axis=1)
    return (
        halves(one) + (np.cos(angle).astype(np.float32), np.sin(angle).astype(np.float32)) + halves(two)
    )


def call(kernel, name, *shapes, scratch=(), in_specs=None):
    outs = tuple(jax.ShapeDtypeStruct(shape, jnp.float32) for shape in shapes)
    return pl.pallas_call(
        kernel,
        out_shape=outs if len(outs) > 1 else outs[0],
        **({} if in_specs is None else {"in_specs": in_specs}),
        scratch_shapes=[
            pltpu.VMEM(shape, jnp.float32) if isinstance(shape, tuple) else shape
            for shape in scratch
        ],
        compiler_params=PARAMS,
        name=name,
    )


def near_pairs(count):
    return [(i, i ^ 1) for i in range(count)]


def far_pairs(count):
    return [(i, (i + (1 if i % 2 else -1)) % count) for i in range(count)]


def swap(near, far, axis, count):
    near = lax.ppermute(near, axis, near_pairs(count))
    far = lax.ppermute(far, axis, far_pairs(count))
    return near, far


def exchange(rows, axis, count, first):
    members = [(first + i) % count for i in range(count)]
    return lax.all_to_all(
        rows, axis, split_axis=0, concat_axis=0, tiled=True, axis_index_groups=[members]
    )


def shards(populations, fluid_mask):
    block = (LAYERS, COLUMNS, HEIGHT)
    z_edge = (Z_ROWS, HEIGHT)
    x_edge = (X_ROWS, HEIGHT)
    relaxed, far, near = call(
        collide_kernel,
        "collide",
        (20,) + block,
        z_edge,
        z_edge,
        in_specs=[pl.BlockSpec(memory_space=pltpu.HBM)] * 2,
        scratch=(
            (19,) + block,
            pltpu.VMEM(block, jnp.int32),
            z_edge,
            z_edge,
            pltpu.SemaphoreType.DMA((LAYERS + 1,)),
        ),
    )(
        pltpu.with_memory_space_constraint(populations, pltpu.HBM),
        pltpu.with_memory_space_constraint(fluid_mask, pltpu.HBM),
    )
    z_near, z_far = swap(near, far, "gz", DEVICES_Z)
    far, near = call(face_kernel, "faces", x_edge, x_edge, scratch=(z_edge, z_edge, x_edge, x_edge))(
        relaxed, z_far, z_near
    )
    x_near, x_far = swap(near, far, "gx", DEVICES_X)
    sums = call(
        step_kernel,
        "steps",
        (8 * DEVICES_X, HEIGHT),
        scratch=(
            (20, LAYERS, RING, HEIGHT),
            (19, LAYERS, RING, HEIGHT),
            (HEIGHT, HEIGHT),
            z_edge,
            z_edge,
            x_edge,
            x_edge,
        ),
    )(relaxed, z_far, z_near, x_far, x_near)
    lines = exchange(sums, "gx", DEVICES_X, FIRST_X)
    spectrum = call(along_x_kernel, "along_x", (4 * DEVICES_Z, HEIGHT))(lines, *x_table())
    spectrum = exchange(spectrum, "gz", DEVICES_Z, FIRST_Z)
    return call(along_z_kernel, "along_z", (2, 4, 4, NZ))(spectrum, *z_tables())


def solution(mesh):
    placed = (P(None, "gx", "gz", None), P("gx", "gz", None))
    return jax.shard_map(
        shards, mesh=mesh, in_specs=placed, out_specs=P(None, "gx", "gz", None), check_vma=False
    )
```

```python
import math

import jax
import jax.numpy as jnp
import ml_dtypes
import numpy as np
from jax import lax
from jax.experimental import pallas as pl
from jax.experimental.pallas import tpu as pltpu
from jax.sharding import PartitionSpec as P

VELOCITIES = (
    (0, 0, 0),
    (1, 0, 0),
    (-1, 0, 0),
    (0, 1, 0),
    (0, -1, 0),
    (0, 0, 1),
    (0, 0, -1),
    (1, 1, 0),
    (-1, -1, 0),
    (1, -1, 0),
    (-1, 1, 0),
    (1, 0, 1),
    (-1, 0, -1),
    (1, 0, -1),
    (-1, 0, 1),
    (0, 1, 1),
    (0, -1, -1),
    (0, 1, -1),
    (0, -1, 1),
)
WEIGHTS = (1.0 / 3.0,) + (1.0 / 18.0,) * 6 + (1.0 / 36.0,) * 12
OPPOSITES = (0, 2, 1, 4, 3, 6, 5, 8, 7, 10, 9, 12, 11, 14, 13, 16, 15, 18, 17)
OMEGA = 1.0 / 0.6
BODY_FORCE = 0.0001
SPEED_UNIT = 0.05

DEVICES_X = 32
DEVICES_Z = 32
LAYERS = 4
COLUMNS = 16
HEIGHT = 128
NX = 128
NZ = 512
MASK = 19
RING = 24
FIRST_X = 18
SLOT = (0, 2, 3, 1)
ORDER_Z = tuple((21 + i) % 32 for i in range(32))

X_UP = tuple(i for i in range(19) if VELOCITIES[i][0] == 1)
X_DOWN = tuple(i for i in range(19) if VELOCITIES[i][0] == -1)
Z_UP = tuple(i for i in range(19) if VELOCITIES[i][2] == 1)
Z_DOWN = tuple(i for i in range(19) if VELOCITIES[i][2] == -1)
Z_UNITS_UP = tuple((i, 0) for i in range(20)) + tuple((i, 1) for i in Z_UP + (MASK,))
Z_UNITS_DOWN = tuple((i, 0) for i in range(20)) + tuple((i, 1) for i in Z_DOWN + (MASK,))
Z_ROWS = len(Z_UNITS_UP) * LAYERS
X_ROWS = 6 * RING

PARAMS = pltpu.CompilerParams(vmem_limit_bytes=32 * 1024 * 1024)


def relax(current, fluid):
    plus = lambda ids: sum(current[i] for i in ids[1:]) + current[ids[0]]
    right, left = plus(X_UP), plus(X_DOWN)
    rho = plus(tuple(i for i in range(19) if VELOCITIES[i][0] == 0)) + right + left
    flow_x = right - left
    flow_y = plus(tuple(i for i in range(19) if VELOCITIES[i][1] == 1)) - plus(
        tuple(i for i in range(19) if VELOCITIES[i][1] == -1)
    )
    flow_z = plus(Z_UP) - plus(Z_DOWN)
    inverse = 1.0 / rho
    ux, uy, uz = flow_x * inverse, flow_y * inverse, flow_z * inverse
    scaled = rho * OMEGA
    rest = scaled * (1.0 - 1.5 * (ux * ux + uy * uy + uz * uz))
    odd_scale = 3.0 * scaled
    even_scale = 4.5 * scaled
    push = (3.0 * BODY_FORCE) * rho
    out = [None] * 19
    keep = 1.0 - OMEGA
    out[0] = jnp.where(fluid, keep * current[0] + WEIGHTS[0] * rest, current[0])
    for i in range(1, 19, 2):
        cx, cy, cz = VELOCITIES[i]
        parts = [u if c == 1 else -u for c, u in ((cx, ux), (cy, uy), (cz, uz)) if c]
        along = parts[0] if len(parts) == 1 else parts[0] + parts[1]
        even = WEIGHTS[i] * (rest + even_scale * (along * along))
        odd = odd_scale * along
        if cx:
            odd = odd + push if cx == 1 else odd - push
        odd = WEIGHTS[i] * odd
        j = OPPOSITES[i]
        out[i] = jnp.where(fluid, keep * current[i] + (even + odd), current[i])
        out[j] = jnp.where(fluid, keep * current[j] + (even - odd), current[j])
    return out


def even_index(axis):
    return lax.axis_index(axis) % 2 == 0


def collide_kernel(pop, mask, relaxed, far, near, held, solid, up, down, arrivals):
    copies = [
        pltpu.make_async_copy(pop.at[:, x], held.at[:, x], arrivals.at[x]) for x in range(LAYERS)
    ]
    copies.append(pltpu.make_async_copy(mask, solid, arrivals.at[LAYERS]))
    for copy in copies:
        copy.start()
    copies[LAYERS].wait()
    for x in range(LAYERS):
        copies[x].wait()
        fluid_here = solid[x].astype(jnp.float32)
        out = relax([held[i, x] for i in range(19)], fluid_here > 0) + [fluid_here]
        for i in range(20):
            relaxed[i, x] = out[i]
        for send, units, edge, step in (
            (up, Z_UNITS_UP, COLUMNS - 1, -1),
            (down, Z_UNITS_DOWN, 0, 1),
        ):
            for u, (i, depth) in enumerate(units):
                z = edge + step * depth
                send[u * LAYERS + x : u * LAYERS + x + 1, :] = out[i][z : z + 1, :]
    even = even_index("gz")
    near[...] = jnp.where(even, up[...], down[...])
    far[...] = jnp.where(even, down[...], up[...])


def ring_tile(i, x, below, above, row):
    one = lambda ref, u: jnp.broadcast_to(ref[u * LAYERS + x : u * LAYERS + x + 1, :], (8, HEIGHT))
    tile = jnp.where(row < 4, one(above, i), one(below, i))
    if (i, 1) in Z_UNITS_DOWN:
        tile = jnp.where(row == 1, one(above, Z_UNITS_DOWN.index((i, 1))), tile)
    if (i, 1) in Z_UNITS_UP:
        tile = jnp.where(row == 6, one(below, Z_UNITS_UP.index((i, 1))), tile)
    return tile


def face_kernel(relaxed, z_far, z_near, far, near, below, above, right, left):
    even = even_index("gz")
    below[...] = jnp.where(even, z_far[...], z_near[...])
    above[...] = jnp.where(even, z_near[...], z_far[...])
    row = lax.broadcasted_iota(jnp.int32, (8, HEIGHT), 0)
    for send, ids, x in ((right, X_UP, LAYERS - 1), (left, X_DOWN, 0)):
        for v, i in enumerate(ids + (MASK,)):
            send[v * RING : v * RING + COLUMNS, :] = relaxed[i, x]
            send[v * RING + COLUMNS : (v + 1) * RING, :] = ring_tile(i, x, below, above, row)
    even = even_index("gx")
    near[...] = jnp.where(even, right[...], left[...])
    far[...] = jnp.where(even, left[...], right[...])


def moved(value, cy, cz):
    if cz:
        value = pltpu.roll(value, cz % RING, 0)
    if cy:
        value = pltpu.roll(value, cy % HEIGHT, 1)
    return value


def fluid_moved(value, cy, cz, lane):
    value = moved(value, cy, cz)
    if cy:
        value = jnp.where(lane == (0 if cy == 1 else HEIGHT - 1), 0.0, value)
    return value > 0


def advance(x, source, own, store):
    lane = lax.broadcasted_iota(jnp.int32, (RING, HEIGHT), 1)
    fluid = source(MASK, x) > 0
    arrived = [own(0, x)]
    for i in range(1, 19):
        cx, cy, cz = VELOCITIES[i]
        open_path = fluid_moved(source(MASK, x - cx), cy, cz, lane)
        value = jnp.where(open_path, moved(source(i, x - cx), cy, cz), own(OPPOSITES[i], x))
        arrived.append(jnp.where(fluid, value, own(i, x)))
    for i, value in enumerate(relax(arrived, fluid)):
        store[i] = value


def inner_kernel(relaxed, z_far, z_near, first, second, below, above):
    even = even_index("gz")
    below[...] = jnp.where(even, z_far[...], z_near[...])
    above[...] = jnp.where(even, z_near[...], z_far[...])
    row = lax.broadcasted_iota(jnp.int32, (8, HEIGHT), 0)
    for i in range(20):
        for x in range(LAYERS):
            first[i, x, 0:COLUMNS] = relaxed[i, x]
            first[i, x, COLUMNS:RING] = ring_tile(i, x, below, above, row)
    read = lambda i, x: first[i, x]
    for x in range(1, LAYERS - 1):
        advance(x, read, read, second.at[:, x - 1])


def outer_kernel(first, inner, x_far, x_near, out, outer, planes, from_left, from_right):
    even = even_index("gx")
    from_left[...] = jnp.where(even, x_far[...], x_near[...])
    from_right[...] = jnp.where(even, x_near[...], x_far[...])
    lane = lax.broadcasted_iota(jnp.int32, (RING, HEIGHT), 1)

    def face(ref, ids, i):
        v = 5 if i == MASK else ids.index(i)
        return ref[v * RING : (v + 1) * RING, :]

    def source(i, x):
        if x < 0:
            return face(from_left, X_UP, i)
        if x >= LAYERS:
            return face(from_right, X_DOWN, i)
        return first[i, x]

    def second(i, x):
        return outer[i, x // (LAYERS - 1)] if x in (0, LAYERS - 1) else inner[i, x - 1]

    for x in (0, LAYERS - 1):
        advance(x, source, source, outer.at[:, x // (LAYERS - 1)])

    zero = jnp.zeros((RING, HEIGHT), jnp.float32)
    place = lambda slot: slice(slot * COLUMNS, (slot + 1) * COLUMNS)
    for x in range(LAYERS):
        fluid = source(MASK, x) > 0
        groups = {-1: zero, 0: second(0, x), 1: zero}
        for i in range(1, 19):
            cx, cy, cz = VELOCITIES[i]
            open_path = fluid_moved(source(MASK, x - cx), cy, cz, lane)
            inside = 0 <= x - cx < LAYERS
            value = moved(second(i, x - cx), cy, cz) if inside else zero
            groups[cx] = groups[cx] + jnp.where(open_path, value, second(OPPOSITES[i], x))
        number = jnp.where(fluid, groups[1] - groups[-1], 0.0)[0:COLUMNS]
        density = jnp.where(fluid, groups[0] + groups[1] + groups[-1], 1.0)[0:COLUMNS]
        if x in (0, LAYERS - 1):
            planes[place(SLOT[x]), :] = number
            planes[place(SLOT[x] + 4), :] = density
        else:
            planes[place(SLOT[x]), :] = number / density
    for slot, ids, x, target in ((6, X_DOWN, 0, -1), (7, X_UP, LAYERS - 1, LAYERS)):
        total = zero
        for i in ids:
            _, cy, cz = VELOCITIES[i]
            open_path = fluid_moved(source(MASK, x), cy, cz, lane)
            total = total + jnp.where(open_path, moved(second(i, x), cy, cz), 0.0)
        total = jnp.where(source(MASK, target) > 0, total, 0.0)
        planes[place(slot), :] = total[0:COLUMNS]
    turned = jnp.transpose(planes[...])
    start = 4 * FIRST_X
    out[0 : HEIGHT - start, :] = turned[start:]
    out[HEIGHT - start :, :] = turned[:start]


def split(value):
    high = value.astype(jnp.bfloat16)
    return high, (value - high.astype(jnp.float32)).astype(jnp.bfloat16)


def dot(a, b):
    return jnp.dot(a, b, preferred_element_type=jnp.float32)


def product(a, b):
    (a_high, a_low), (b_high, b_low) = a, b
    return dot(a_high, b_high) + (dot(a_high, b_low) + dot(a_low, b_high))


def along_x_kernel(got, high, low, out):
    lane = lax.broadcasted_iota(jnp.int32, (DEVICES_X, HEIGHT), 1)
    within = lambda slot: (lane >= slot * COLUMNS) & (lane < (slot + 1) * COLUMNS)
    speeds = []
    for y in range(4):
        own = got[pl.ds(y, DEVICES_X, stride=4), :]
        from_left = pltpu.roll(own, 1, 0)
        from_right = pltpu.roll(own, DEVICES_X - 1, 0)
        total = own + jnp.where(within(0), pltpu.roll(from_left, 16, 1), 0.0)
        total = total + jnp.where(within(4), pltpu.roll(from_left, 80, 1), 0.0)
        total = total - jnp.where(within(1), pltpu.roll(from_right, 48, 1), 0.0)
        total = total + jnp.where(within(5), pltpu.roll(from_right, 112, 1), 0.0)
        density = jnp.where(lane < 2 * COLUMNS, pltpu.roll(total, 64, 1), 1.0)
        speeds.append(total / density)
    blocks = []
    for shift in (0, 64):
        for x in range(4):
            block = jnp.zeros((DEVICES_X, HEIGHT), jnp.float32)
            for y in range(4):
                start = shift + COLUMNS * y
                piece = pltpu.roll(speeds[y], (start - COLUMNS * SLOT[x]) % HEIGHT, 1)
                block = jnp.where((lane >= start) & (lane < start + COLUMNS), piece, block)
            blocks.append(block)
    lines = jnp.concatenate(blocks, axis=0)
    result = product((high[...], low[...]), split(lines))
    for r in range(4):
        out[pl.ds(r, DEVICES_Z, stride=4), :] = result[32 * r : 32 * r + 32, :]


def along_z_kernel(got, one_high, one_low, twist_cos, twist_sin, two_high, two_low, out):
    rows = [got[pl.ds(r, DEVICES_Z, stride=4), :] for r in range(4)]
    lines = jnp.concatenate(
        [
            jnp.concatenate([rows[0], rows[1]], axis=1),
            jnp.concatenate([rows[2], rows[3]], axis=1),
        ],
        axis=0,
    )
    inner = product((one_high[...], one_low[...]), split(lines))
    real, imag = inner[0:32], inner[32:64]
    cosine, sine = twist_cos[...], twist_sin[...]
    turned = jnp.concatenate([real * cosine + imag * sine, imag * cosine - real * sine], axis=0)
    both = product(split(turned), (two_high[...], two_low[...]))
    outer_real = both[0:32, 0:256] + both[32:64, 256:512]
    outer_imag = both[32:64, 0:256] - both[0:32, 256:512]
    for c, value in enumerate((outer_real, outer_imag)):
        columns = jnp.transpose(value)
        wide = columns.reshape(16, 16, 32)
        for quad in range(4):
            parts = [wide[:, 4 * quad + k, :] for k in range(4)]
            tile = jnp.concatenate(parts, axis=1)
            for y in range(4):
                out[c, y, :, 128 * quad : 128 * quad + 128] = tile[4 * y : 4 * y + 4]


def halves(table):
    table = np.asarray(table, np.float32)
    high = table.astype(ml_dtypes.bfloat16)
    low = (table - high.astype(np.float32)).astype(ml_dtypes.bfloat16)
    return high, low


def x_table():
    part, pair, block = np.meshgrid(np.arange(2), np.arange(2), np.arange(32), indexing="ij")
    odd, inner, outer = np.meshgrid(np.arange(2), np.arange(4), np.arange(32), indexing="ij")
    kx = (4 * (np.asarray(ORDER_Z)[block]) + 2 * pair).reshape(-1, 1) + odd.reshape(1, -1)
    x = (4 * ((outer + FIRST_X) % 32) + inner).reshape(1, -1)
    angle = 2.0 * np.pi * ((kx * x) % NX) / NX
    scale = 1.0 / (math.sqrt(NX * NZ) * SPEED_UNIT)
    return halves(np.where(part.reshape(-1, 1) == 0, np.cos(angle), -np.sin(angle)) * scale)


def z_tables():
    k, b = np.meshgrid(np.arange(32), np.asarray(ORDER_Z), indexing="ij")
    angle = 2.0 * np.pi * ((k * b) % 32) / 32
    one = np.block([[np.cos(angle), np.sin(angle)], [-np.sin(angle), np.cos(angle)]])
    angle = 2.0 * np.pi * (np.arange(32)[:, None] * (np.arange(256) % 16)[None, :]) / NZ
    pair, odd, y, z = (v.reshape(-1, 1) for v in np.unravel_index(np.arange(256), (2, 2, 4, 16)))
    y_out, kx_out, k_out = (v.reshape(1, -1) for v in np.unravel_index(np.arange(256), (4, 4, 16)))
    same = (y == y_out) & (2 * pair + odd == kx_out)
    turn = 2.0 * np.pi * ((z * k_out) % 16) / 16
    two = np.concatenate([same * np.cos(turn), same * np.sin(turn)], axis=1)
    return (
        halves(one) + (np.cos(angle).astype(np.float32), np.sin(angle).astype(np.float32)) + halves(two)
    )


def call(kernel, name, *shapes, scratch=(), in_specs=None):
    outs = tuple(jax.ShapeDtypeStruct(shape, jnp.float32) for shape in shapes)
    return pl.pallas_call(
        kernel,
        out_shape=outs if len(outs) > 1 else outs[0],
        **({} if in_specs is None else {"in_specs": in_specs}),
        scratch_shapes=[
            pltpu.VMEM(shape, jnp.float32) if isinstance(shape, tuple) else shape
            for shape in scratch
        ],
        compiler_params=PARAMS,
        name=name,
    )


def near_pairs(count):
    return [(i, i ^ 1) for i in range(count)]


def far_pairs(count):
    return [(i, (i + (1 if i % 2 else -1)) % count) for i in range(count)]


def swap(near, far, axis, count):
    near = lax.ppermute(near, axis, near_pairs(count))
    far = lax.ppermute(far, axis, far_pairs(count))
    return near, far


def exchange(rows, axis, members):
    return lax.all_to_all(
        rows, axis, split_axis=0, concat_axis=0, tiled=True, axis_index_groups=[members]
    )


def shards(populations, fluid_mask):
    block = (LAYERS, COLUMNS, HEIGHT)
    z_edge = (Z_ROWS, HEIGHT)
    x_edge = (X_ROWS, HEIGHT)
    relaxed, far, near = call(
        collide_kernel,
        "collide",
        (20,) + block,
        z_edge,
        z_edge,
        in_specs=[pl.BlockSpec(memory_space=pltpu.HBM)] * 2,
        scratch=(
            (19,) + block,
            pltpu.VMEM(block, jnp.int32),
            z_edge,
            z_edge,
            pltpu.SemaphoreType.DMA((LAYERS + 1,)),
        ),
    )(
        pltpu.with_memory_space_constraint(populations, pltpu.HBM),
        pltpu.with_memory_space_constraint(fluid_mask, pltpu.HBM),
    )
    z_near, z_far = swap(near, far, "gz", DEVICES_Z)
    far, near = call(face_kernel, "faces", x_edge, x_edge, scratch=(z_edge, z_edge, x_edge, x_edge))(
        relaxed, z_far, z_near
    )
    x_near, x_far = swap(near, far, "gx", DEVICES_X)
    ring_block = (LAYERS, RING, HEIGHT)
    first, inner = call(
        inner_kernel, "inner", (20,) + ring_block, (19, 2, RING, HEIGHT), scratch=(z_edge, z_edge)
    )(relaxed, z_far, z_near)
    sums = call(
        outer_kernel,
        "outer",
        (HEIGHT, HEIGHT),
        scratch=((19, 2, RING, HEIGHT), (HEIGHT, HEIGHT), x_edge, x_edge),
    )(first, inner, x_far, x_near)
    lines = exchange(sums, "gx", [(FIRST_X + i) % DEVICES_X for i in range(DEVICES_X)])
    spectrum = call(along_x_kernel, "along_x", (4 * DEVICES_Z, HEIGHT))(lines, *x_table())
    spectrum = exchange(spectrum, "gz", list(ORDER_Z))
    return call(along_z_kernel, "along_z", (2, 4, 4, NZ))(spectrum, *z_tables())


def solution(mesh):
    placed = (P(None, "gx", "gz", None), P("gx", "gz", None))
    return jax.shard_map(
        shards, mesh=mesh, in_specs=placed, out_specs=P(None, "gx", "gz", None), check_vma=False
    )
```

```python
import math

import jax
import jax.numpy as jnp
import ml_dtypes
import numpy as np
from jax import lax
from jax.experimental import pallas as pl
from jax.experimental.pallas import tpu as pltpu
from jax.sharding import PartitionSpec as P

VELOCITIES = (
    (0, 0, 0),
    (1, 0, 0),
    (-1, 0, 0),
    (0, 1, 0),
    (0, -1, 0),
    (0, 0, 1),
    (0, 0, -1),
    (1, 1, 0),
    (-1, -1, 0),
    (1, -1, 0),
    (-1, 1, 0),
    (1, 0, 1),
    (-1, 0, -1),
    (1, 0, -1),
    (-1, 0, 1),
    (0, 1, 1),
    (0, -1, -1),
    (0, 1, -1),
    (0, -1, 1),
)
WEIGHTS = (1.0 / 3.0,) + (1.0 / 18.0,) * 6 + (1.0 / 36.0,) * 12
OPPOSITES = (0, 2, 1, 4, 3, 6, 5, 8, 7, 10, 9, 12, 11, 14, 13, 16, 15, 18, 17)
OMEGA = 1.0 / 0.6
BODY_FORCE = 0.0001
SPEED_UNIT = 0.05

DEVICES_X = 32
DEVICES_Z = 32
LAYERS = 4
COLUMNS = 16
HEIGHT = 128
NX = 128
NZ = 512
MASK = 19
RING = 24
FIRST_X = 18
SLOT = (0, 2, 3, 1)
ORDER_Z = tuple((21 + i) % 32 for i in range(32))

X_UP = tuple(i for i in range(19) if VELOCITIES[i][0] == 1)
X_DOWN = tuple(i for i in range(19) if VELOCITIES[i][0] == -1)
Z_UP = tuple(i for i in range(19) if VELOCITIES[i][2] == 1)
Z_DOWN = tuple(i for i in range(19) if VELOCITIES[i][2] == -1)
Z_UNITS_UP = tuple((i, 0) for i in range(20)) + tuple((i, 1) for i in Z_UP + (MASK,))
Z_UNITS_DOWN = tuple((i, 0) for i in range(20)) + tuple((i, 1) for i in Z_DOWN + (MASK,))
Z_ROWS = len(Z_UNITS_UP) * LAYERS
X_ROWS = 6 * RING

PARAMS = pltpu.CompilerParams(vmem_limit_bytes=32 * 1024 * 1024)


def relax(current, fluid):
    plus = lambda ids: sum(current[i] for i in ids[1:]) + current[ids[0]]
    right, left = plus(X_UP), plus(X_DOWN)
    rho = plus(tuple(i for i in range(19) if VELOCITIES[i][0] == 0)) + right + left
    flow_x = right - left
    flow_y = plus(tuple(i for i in range(19) if VELOCITIES[i][1] == 1)) - plus(
        tuple(i for i in range(19) if VELOCITIES[i][1] == -1)
    )
    flow_z = plus(Z_UP) - plus(Z_DOWN)
    inverse = 1.0 / rho
    ux, uy, uz = flow_x * inverse, flow_y * inverse, flow_z * inverse
    scaled = rho * OMEGA
    rest = scaled * (1.0 - 1.5 * (ux * ux + uy * uy + uz * uz))
    odd_scale = 3.0 * scaled
    even_scale = 4.5 * scaled
    push = (3.0 * BODY_FORCE) * rho
    out = [None] * 19
    keep = 1.0 - OMEGA
    out[0] = jnp.where(fluid, keep * current[0] + WEIGHTS[0] * rest, current[0])
    for i in range(1, 19, 2):
        cx, cy, cz = VELOCITIES[i]
        parts = [u if c == 1 else -u for c, u in ((cx, ux), (cy, uy), (cz, uz)) if c]
        along = parts[0] if len(parts) == 1 else parts[0] + parts[1]
        even = WEIGHTS[i] * (rest + even_scale * (along * along))
        odd = odd_scale * along
        if cx:
            odd = odd + push if cx == 1 else odd - push
        odd = WEIGHTS[i] * odd
        j = OPPOSITES[i]
        out[i] = jnp.where(fluid, keep * current[i] + (even + odd), current[i])
        out[j] = jnp.where(fluid, keep * current[j] + (even - odd), current[j])
    return out


def even_index(axis):
    return lax.axis_index(axis) % 2 == 0


def collide_kernel(pop, mask, relaxed, far, near, held, solid, up, down, arrivals):
    copies = [
        pltpu.make_async_copy(pop.at[:, x], held.at[:, x], arrivals.at[x]) for x in range(LAYERS)
    ]
    copies.append(pltpu.make_async_copy(mask, solid, arrivals.at[LAYERS]))
    for copy in copies[::-1]:
        copy.start()
    copies[LAYERS].wait()
    for x in range(LAYERS)[::-1]:
        copies[x].wait()
        fluid_here = solid[x].astype(jnp.float32)
        out = relax([held[i, x] for i in range(19)], fluid_here > 0) + [fluid_here]
        for i in range(20):
            relaxed[i, x] = out[i]
        for send, units, edge, step in (
            (up, Z_UNITS_UP, COLUMNS - 1, -1),
            (down, Z_UNITS_DOWN, 0, 1),
        ):
            for u, (i, depth) in enumerate(units):
                z = edge + step * depth
                send[u * LAYERS + x : u * LAYERS + x + 1, :] = out[i][z : z + 1, :]
    even = even_index("gz")
    near[...] = jnp.where(even, up[...], down[...])
    far[...] = jnp.where(even, down[...], up[...])


def ring_tile(i, x, below, above, row):
    one = lambda ref, u: jnp.broadcast_to(ref[u * LAYERS + x : u * LAYERS + x + 1, :], (8, HEIGHT))
    tile = jnp.where(row < 4, one(above, i), one(below, i))
    if (i, 1) in Z_UNITS_DOWN:
        tile = jnp.where(row == 1, one(above, Z_UNITS_DOWN.index((i, 1))), tile)
    if (i, 1) in Z_UNITS_UP:
        tile = jnp.where(row == 6, one(below, Z_UNITS_UP.index((i, 1))), tile)
    return tile


def face_kernel(relaxed, z_far, z_near, far, near, below, above, right, left):
    even = even_index("gz")
    below[...] = jnp.where(even, z_far[...], z_near[...])
    above[...] = jnp.where(even, z_near[...], z_far[...])
    row = lax.broadcasted_iota(jnp.int32, (8, HEIGHT), 0)
    for send, ids, x in ((right, X_UP, LAYERS - 1), (left, X_DOWN, 0)):
        for v, i in enumerate(ids + (MASK,)):
            send[v * RING : v * RING + COLUMNS, :] = relaxed[i, x]
            send[v * RING + COLUMNS : (v + 1) * RING, :] = ring_tile(i, x, below, above, row)
    even = even_index("gx")
    near[...] = jnp.where(even, right[...], left[...])
    far[...] = jnp.where(even, left[...], right[...])


def moved(value, cy, cz):
    if cz:
        value = pltpu.roll(value, cz % RING, 0)
    if cy:
        value = pltpu.roll(value, cy % HEIGHT, 1)
    return value


def fluid_moved(value, cy, cz, lane):
    value = moved(value, cy, cz)
    if cy:
        value = jnp.where(lane == (0 if cy == 1 else HEIGHT - 1), 0.0, value)
    return value > 0


def advance(x, source, own, store):
    lane = lax.broadcasted_iota(jnp.int32, (RING, HEIGHT), 1)
    fluid = source(MASK, x) > 0
    arrived = [own(0, x)]
    for i in range(1, 19):
        cx, cy, cz = VELOCITIES[i]
        open_path = fluid_moved(source(MASK, x - cx), cy, cz, lane)
        value = jnp.where(open_path, moved(source(i, x - cx), cy, cz), own(OPPOSITES[i], x))
        arrived.append(jnp.where(fluid, value, own(i, x)))
    for i, value in enumerate(relax(arrived, fluid)):
        store[i] = value


def inner_kernel(relaxed, z_far, z_near, first, second, below, above):
    even = even_index("gz")
    below[...] = jnp.where(even, z_far[...], z_near[...])
    above[...] = jnp.where(even, z_near[...], z_far[...])
    row = lax.broadcasted_iota(jnp.int32, (8, HEIGHT), 0)
    for i in range(20):
        for x in range(LAYERS):
            first[i, x, 0:COLUMNS] = relaxed[i, x]
            first[i, x, COLUMNS:RING] = ring_tile(i, x, below, above, row)
    read = lambda i, x: first[i, x]
    for x in range(1, LAYERS - 1):
        advance(x, read, read, second.at[:, x - 1])


def outer_kernel(first, inner, x_far, x_near, out, outer, planes, from_left, from_right):
    even = even_index("gx")
    from_left[...] = jnp.where(even, x_far[...], x_near[...])
    from_right[...] = jnp.where(even, x_near[...], x_far[...])
    lane = lax.broadcasted_iota(jnp.int32, (RING, HEIGHT), 1)

    def face(ref, ids, i):
        v = 5 if i == MASK else ids.index(i)
        return ref[v * RING : (v + 1) * RING, :]

    def source(i, x):
        if x < 0:
            return face(from_left, X_UP, i)
        if x >= LAYERS:
            return face(from_right, X_DOWN, i)
        return first[i, x]

    def second(i, x):
        return outer[i, x // (LAYERS - 1)] if x in (0, LAYERS - 1) else inner[i, x - 1]

    for x in (0, LAYERS - 1):
        advance(x, source, source, outer.at[:, x // (LAYERS - 1)])

    zero = jnp.zeros((RING, HEIGHT), jnp.float32)
    place = lambda slot: slice(slot * COLUMNS, (slot + 1) * COLUMNS)
    for x in range(LAYERS):
        fluid = source(MASK, x) > 0
        groups = {-1: zero, 0: second(0, x), 1: zero}
        for i in range(1, 19):
            cx, cy, cz = VELOCITIES[i]
            open_path = fluid_moved(source(MASK, x - cx), cy, cz, lane)
            inside = 0 <= x - cx < LAYERS
            value = moved(second(i, x - cx), cy, cz) if inside else zero
            groups[cx] = groups[cx] + jnp.where(open_path, value, second(OPPOSITES[i], x))
        number = jnp.where(fluid, groups[1] - groups[-1], 0.0)[0:COLUMNS]
        density = jnp.where(fluid, groups[0] + groups[1] + groups[-1], 1.0)[0:COLUMNS]
        if x in (0, LAYERS - 1):
            planes[place(SLOT[x]), :] = number
            planes[place(SLOT[x] + 4), :] = density
        else:
            planes[place(SLOT[x]), :] = number / density
    for slot, ids, x, target in ((6, X_DOWN, 0, -1), (7, X_UP, LAYERS - 1, LAYERS)):
        total = zero
        for i in ids:
            _, cy, cz = VELOCITIES[i]
            open_path = fluid_moved(source(MASK, x), cy, cz, lane)
            total = total + jnp.where(open_path, moved(second(i, x), cy, cz), 0.0)
        total = jnp.where(source(MASK, target) > 0, total, 0.0)
        planes[place(slot), :] = total[0:COLUMNS]
    turned = jnp.transpose(planes[...])
    start = 4 * FIRST_X
    out[0 : HEIGHT - start, :] = turned[start:]
    out[HEIGHT - start :, :] = turned[:start]


def split(value):
    high = value.astype(jnp.bfloat16)
    return high, (value - high.astype(jnp.float32)).astype(jnp.bfloat16)


def dot(a, b):
    return jnp.dot(a, b, preferred_element_type=jnp.float32)


def times_split(stacked, value):
    high, low = split(value)
    count = stacked.shape[0] // 2
    both = dot(stacked, high)
    return both[:count] + (both[count:] + dot(stacked[:count], low))


def split_times(value, high, low):
    stacked = jnp.concatenate(split(value), axis=0)
    count = value.shape[0]
    both = dot(stacked, high)
    return both[:count] + (both[count:] + dot(stacked[:count], low))


def along_x_kernel(got, table, out):
    lane = lax.broadcasted_iota(jnp.int32, (DEVICES_X, HEIGHT), 1)
    within = lambda slot: (lane >= slot * COLUMNS) & (lane < (slot + 1) * COLUMNS)
    speeds = []
    for y in range(4):
        own = got[pl.ds(y, DEVICES_X, stride=4), :]
        from_left = pltpu.roll(own, 1, 0)
        from_right = pltpu.roll(own, DEVICES_X - 1, 0)
        total = own + jnp.where(within(0), pltpu.roll(from_left, 16, 1), 0.0)
        total = total + jnp.where(within(4), pltpu.roll(from_left, 80, 1), 0.0)
        total = total - jnp.where(within(1), pltpu.roll(from_right, 48, 1), 0.0)
        total = total + jnp.where(within(5), pltpu.roll(from_right, 112, 1), 0.0)
        density = jnp.where(lane < 2 * COLUMNS, pltpu.roll(total, 64, 1), 1.0)
        speeds.append(total / density)
    blocks = []
    for x in range(4):
        block = jnp.zeros((DEVICES_X, HEIGHT), jnp.float32)
        for y in range(4):
            piece = pltpu.roll(speeds[y], (COLUMNS * (y - SLOT[x])) % HEIGHT, 1)
            block = jnp.where(within(y), piece, block)
        blocks.append(block)
    blocks += [pltpu.roll(block, 64, 1) for block in blocks]
    lines = jnp.concatenate(blocks, axis=0)
    result = times_split(table[...], lines)
    for r in range(4):
        out[pl.ds(r, DEVICES_Z, stride=4), :] = result[32 * r : 32 * r + 32, :]


def along_z_kernel(got, one, twist_cos, twist_sin, two_high, two_low, out):
    rows = [got[pl.ds(r, DEVICES_Z, stride=4), :] for r in range(4)]
    lines = jnp.concatenate(
        [
            jnp.concatenate([rows[0], rows[1]], axis=1),
            jnp.concatenate([rows[2], rows[3]], axis=1),
        ],
        axis=0,
    )
    inner = times_split(one[...], lines)
    real, imag = inner[0:32], inner[32:64]
    cosine, sine = twist_cos[...], twist_sin[...]
    turned = jnp.concatenate([real * cosine + imag * sine, imag * cosine - real * sine], axis=0)
    both = split_times(turned, two_high[...], two_low[...])
    outer_real = both[0:32, 0:256] + both[32:64, 256:512]
    outer_imag = both[32:64, 0:256] - both[0:32, 256:512]
    for c, value in enumerate((outer_real, outer_imag)):
        columns = jnp.transpose(value)
        for quad in range(4):
            parts = [columns[16 * k : 16 * k + 16] for k in range(4 * quad, 4 * quad + 4)]
            tile = jnp.concatenate(parts, axis=1)
            for y in range(4):
                out[c, y, :, 128 * quad : 128 * quad + 128] = tile[4 * y : 4 * y + 4]


def halves(table):
    table = np.asarray(table, np.float32)
    high = table.astype(ml_dtypes.bfloat16)
    low = (table - high.astype(np.float32)).astype(ml_dtypes.bfloat16)
    return high, low


def x_table():
    part, pair, block = np.meshgrid(np.arange(2), np.arange(2), np.arange(32), indexing="ij")
    odd, inner, outer = np.meshgrid(np.arange(2), np.arange(4), np.arange(32), indexing="ij")
    kx = (4 * (np.asarray(ORDER_Z)[block]) + 2 * pair).reshape(-1, 1) + odd.reshape(1, -1)
    x = (4 * ((outer + FIRST_X) % 32) + inner).reshape(1, -1)
    angle = 2.0 * np.pi * ((kx * x) % NX) / NX
    scale = 1.0 / (math.sqrt(NX * NZ) * SPEED_UNIT)
    table = halves(np.where(part.reshape(-1, 1) == 0, np.cos(angle), -np.sin(angle)) * scale)
    return np.concatenate(table, axis=0)


def z_tables():
    k, b = np.meshgrid(np.arange(32), np.asarray(ORDER_Z), indexing="ij")
    angle = 2.0 * np.pi * ((k * b) % 32) / 32
    one = np.block([[np.cos(angle), np.sin(angle)], [-np.sin(angle), np.cos(angle)]])
    angle = 2.0 * np.pi * (np.arange(32)[:, None] * (np.arange(256) % 16)[None, :]) / NZ
    pair, odd, y, z = (v.reshape(-1, 1) for v in np.unravel_index(np.arange(256), (2, 2, 4, 16)))
    k_out, y_out, kx_out = (v.reshape(1, -1) for v in np.unravel_index(np.arange(256), (16, 4, 4)))
    same = (y == y_out) & (2 * pair + odd == kx_out)
    turn = 2.0 * np.pi * ((z * k_out) % 16) / 16
    two = np.concatenate([same * np.cos(turn), same * np.sin(turn)], axis=1)
    return (
        np.concatenate(halves(one), axis=0),
        np.cos(angle).astype(np.float32),
        np.sin(angle).astype(np.float32),
        *halves(two),
    )


def call(kernel, name, *shapes, scratch=(), in_specs=None):
    outs = tuple(jax.ShapeDtypeStruct(shape, jnp.float32) for shape in shapes)
    return pl.pallas_call(
        kernel,
        out_shape=outs if len(outs) > 1 else outs[0],
        **({} if in_specs is None else {"in_specs": in_specs}),
        scratch_shapes=[
            pltpu.VMEM(shape, jnp.float32) if isinstance(shape, tuple) else shape
            for shape in scratch
        ],
        compiler_params=PARAMS,
        name=name,
    )


def near_pairs(count):
    return [(i, i ^ 1) for i in range(count)]


def far_pairs(count):
    return [(i, (i + (1 if i % 2 else -1)) % count) for i in range(count)]


def swap(near, far, axis, count):
    near = lax.ppermute(near, axis, near_pairs(count))
    far = lax.ppermute(far, axis, far_pairs(count))
    return near, far


def exchange(rows, axis, members):
    return lax.all_to_all(
        rows, axis, split_axis=0, concat_axis=0, tiled=True, axis_index_groups=[members]
    )


def shards(populations, fluid_mask):
    block = (LAYERS, COLUMNS, HEIGHT)
    z_edge = (Z_ROWS, HEIGHT)
    x_edge = (X_ROWS, HEIGHT)
    relaxed, far, near = call(
        collide_kernel,
        "collide",
        (20,) + block,
        z_edge,
        z_edge,
        in_specs=[pl.BlockSpec(memory_space=pltpu.HBM)] * 2,
        scratch=(
            (19,) + block,
            pltpu.VMEM(block, jnp.int32),
            z_edge,
            z_edge,
            pltpu.SemaphoreType.DMA((LAYERS + 1,)),
        ),
    )(
        pltpu.with_memory_space_constraint(populations, pltpu.HBM),
        pltpu.with_memory_space_constraint(fluid_mask, pltpu.HBM),
    )
    z_near, z_far = swap(near, far, "gz", DEVICES_Z)
    far, near = call(face_kernel, "faces", x_edge, x_edge, scratch=(z_edge, z_edge, x_edge, x_edge))(
        relaxed, z_far, z_near
    )
    x_near, x_far = swap(near, far, "gx", DEVICES_X)
    ring_block = (LAYERS, RING, HEIGHT)
    first, inner = call(
        inner_kernel, "inner", (20,) + ring_block, (19, 2, RING, HEIGHT), scratch=(z_edge, z_edge)
    )(relaxed, z_far, z_near)
    sums = call(
        outer_kernel,
        "outer",
        (HEIGHT, HEIGHT),
        scratch=((19, 2, RING, HEIGHT), (HEIGHT, HEIGHT), x_edge, x_edge),
    )(first, inner, x_far, x_near)
    lines = exchange(sums, "gx", [(FIRST_X + i) % DEVICES_X for i in range(DEVICES_X)])
    spectrum = call(along_x_kernel, "along_x", (4 * DEVICES_Z, HEIGHT))(lines, x_table())
    spectrum = exchange(spectrum, "gz", list(ORDER_Z))
    return call(along_z_kernel, "along_z", (2, 4, 4, NZ))(spectrum, *z_tables())


def solution(mesh):
    placed = (P(None, "gx", "gz", None), P("gx", "gz", None))
    return jax.shard_map(
        shards, mesh=mesh, in_specs=placed, out_specs=P(None, "gx", "gz", None), check_vma=False
    )
```

```python
import math

import jax
import jax.numpy as jnp
import ml_dtypes
import numpy as np
from jax import lax
from jax.experimental import pallas as pl
from jax.experimental.pallas import tpu as pltpu
from jax.sharding import PartitionSpec as P

VELOCITIES = (
    (0, 0, 0),
    (1, 0, 0),
    (-1, 0, 0),
    (0, 1, 0),
    (0, -1, 0),
    (0, 0, 1),
    (0, 0, -1),
    (1, 1, 0),
    (-1, -1, 0),
    (1, -1, 0),
    (-1, 1, 0),
    (1, 0, 1),
    (-1, 0, -1),
    (1, 0, -1),
    (-1, 0, 1),
    (0, 1, 1),
    (0, -1, -1),
    (0, 1, -1),
    (0, -1, 1),
)
WEIGHTS = (1.0 / 3.0,) + (1.0 / 18.0,) * 6 + (1.0 / 36.0,) * 12
OPPOSITES = (0, 2, 1, 4, 3, 6, 5, 8, 7, 10, 9, 12, 11, 14, 13, 16, 15, 18, 17)
OMEGA = 1.0 / 0.6
BODY_FORCE = 0.0001
SPEED_UNIT = 0.05

DEVICES_X = 32
DEVICES_Z = 32
LAYERS = 4
COLUMNS = 16
HEIGHT = 128
NX = 128
NZ = 512
MASK = 19
RING = 24
FIRST_X = 18
SLOT = (0, 2, 3, 1)
ORDER_Z = tuple((21 + i) % 32 for i in range(32))

X_UP = tuple(i for i in range(19) if VELOCITIES[i][0] == 1)
X_DOWN = tuple(i for i in range(19) if VELOCITIES[i][0] == -1)
Z_UP = tuple(i for i in range(19) if VELOCITIES[i][2] == 1)
Z_DOWN = tuple(i for i in range(19) if VELOCITIES[i][2] == -1)
SHIFT = 2
DEPTH = tuple(4 if i in Z_DOWN + (MASK,) else 3 for i in range(20))
Z_START = tuple(LAYERS * sum(DEPTH[:i]) for i in range(20))
Z_ROWS = LAYERS * sum(DEPTH)
X_ROWS = 6 * RING

PARAMS = pltpu.CompilerParams(vmem_limit_bytes=32 * 1024 * 1024)


def relax(current, fluid):
    plus = lambda ids: sum(current[i] for i in ids[1:]) + current[ids[0]]
    right, left = plus(X_UP), plus(X_DOWN)
    rho = plus(tuple(i for i in range(19) if VELOCITIES[i][0] == 0)) + right + left
    flow_x = right - left
    flow_y = plus(tuple(i for i in range(19) if VELOCITIES[i][1] == 1)) - plus(
        tuple(i for i in range(19) if VELOCITIES[i][1] == -1)
    )
    flow_z = plus(Z_UP) - plus(Z_DOWN)
    inverse = 1.0 / rho
    ux, uy, uz = flow_x * inverse, flow_y * inverse, flow_z * inverse
    scaled = rho * OMEGA
    rest = scaled * (1.0 - 1.5 * (ux * ux + uy * uy + uz * uz))
    odd_scale = 3.0 * scaled
    even_scale = 4.5 * scaled
    push = (3.0 * BODY_FORCE) * rho
    out = [None] * 19
    keep = 1.0 - OMEGA
    out[0] = jnp.where(fluid, keep * current[0] + WEIGHTS[0] * rest, current[0])
    for i in range(1, 19, 2):
        cx, cy, cz = VELOCITIES[i]
        parts = [u if c == 1 else -u for c, u in ((cx, ux), (cy, uy), (cz, uz)) if c]
        along = parts[0] if len(parts) == 1 else parts[0] + parts[1]
        even = WEIGHTS[i] * (rest + even_scale * (along * along))
        odd = odd_scale * along
        if cx:
            odd = odd + push if cx == 1 else odd - push
        odd = WEIGHTS[i] * odd
        j = OPPOSITES[i]
        out[i] = jnp.where(fluid, keep * current[i] + (even + odd), current[i])
        out[j] = jnp.where(fluid, keep * current[j] + (even - odd), current[j])
    return out


def even_index(axis):
    return lax.axis_index(axis) % 2 == 0


def collide_kernel(pop, mask, relaxed, edge, held, solid, arrivals):
    copies = [
        pltpu.make_async_copy(pop.at[:, x], held.at[:, x], arrivals.at[x]) for x in range(LAYERS)
    ]
    copies.append(pltpu.make_async_copy(mask, solid, arrivals.at[LAYERS]))
    for copy in copies[::-1]:
        copy.start()
    copies[LAYERS].wait()
    for x in range(LAYERS)[::-1]:
        copies[x].wait()
        fluid_here = solid[x].astype(jnp.float32)
        out = relax([held[i, x] for i in range(19)], fluid_here > 0) + [fluid_here]
        for i in range(20):
            relaxed[i, x] = out[i]
            start = Z_START[i] + x * DEPTH[i]
            edge[start : start + DEPTH[i], :] = out[i][0 : DEPTH[i]]


def widen(target, i, x, relaxed, beyond):
    start = Z_START[i] + x * DEPTH[i]
    target[0:COLUMNS] = relaxed[i, x]
    target[COLUMNS:RING] = jnp.zeros((RING - COLUMNS, HEIGHT), jnp.float32)
    target[COLUMNS : COLUMNS + DEPTH[i]] = beyond[start : start + DEPTH[i], :]
    target[...] = pltpu.roll(target[...], RING - SHIFT, 0)


def face_kernel(relaxed, beyond, far, near, right, left):
    for send, ids, x in ((right, X_UP, LAYERS - 1), (left, X_DOWN, 0)):
        for v, i in enumerate(ids + (MASK,)):
            widen(send.at[v * RING : (v + 1) * RING], i, x, relaxed, beyond)
    even = even_index("gx")
    near[...] = jnp.where(even, right[...], left[...])
    far[...] = jnp.where(even, left[...], right[...])


def moved(value, cy, cz):
    if cz:
        value = pltpu.roll(value, cz % RING, 0)
    if cy:
        value = pltpu.roll(value, cy % HEIGHT, 1)
    return value


def fluid_moved(value, cy, cz, lane):
    value = moved(value, cy, cz)
    if cy:
        value = jnp.where(lane == (0 if cy == 1 else HEIGHT - 1), 0.0, value)
    return value > 0


def advance(x, source, own, store):
    lane = lax.broadcasted_iota(jnp.int32, (RING, HEIGHT), 1)
    fluid = source(MASK, x) > 0
    arrived = [own(0, x)]
    for i in range(1, 19):
        cx, cy, cz = VELOCITIES[i]
        open_path = fluid_moved(source(MASK, x - cx), cy, cz, lane)
        value = jnp.where(open_path, moved(source(i, x - cx), cy, cz), own(OPPOSITES[i], x))
        arrived.append(jnp.where(fluid, value, own(i, x)))
    for i, value in enumerate(relax(arrived, fluid)):
        store[i] = value


def inner_kernel(relaxed, beyond, first, second):
    for i in range(20):
        for x in range(LAYERS):
            widen(first.at[i, x], i, x, relaxed, beyond)
    read = lambda i, x: first[i, x]
    for x in range(1, LAYERS - 1):
        advance(x, read, read, second.at[:, x - 1])


def outer_kernel(first, inner, x_far, x_near, out, outer, planes, from_left, from_right):
    even = even_index("gx")
    from_left[...] = jnp.where(even, x_far[...], x_near[...])
    from_right[...] = jnp.where(even, x_near[...], x_far[...])
    lane = lax.broadcasted_iota(jnp.int32, (RING, HEIGHT), 1)

    def face(ref, ids, i):
        v = 5 if i == MASK else ids.index(i)
        return ref[v * RING : (v + 1) * RING, :]

    def source(i, x):
        if x < 0:
            return face(from_left, X_UP, i)
        if x >= LAYERS:
            return face(from_right, X_DOWN, i)
        return first[i, x]

    def second(i, x):
        return outer[i, x // (LAYERS - 1)] if x in (0, LAYERS - 1) else inner[i, x - 1]

    for x in (0, LAYERS - 1):
        advance(x, source, source, outer.at[:, x // (LAYERS - 1)])

    zero = jnp.zeros((RING, HEIGHT), jnp.float32)
    place = lambda slot: slice(slot * COLUMNS, (slot + 1) * COLUMNS)
    for x in range(LAYERS):
        fluid = source(MASK, x) > 0
        groups = {-1: zero, 0: second(0, x), 1: zero}
        for i in range(1, 19):
            cx, cy, cz = VELOCITIES[i]
            open_path = fluid_moved(source(MASK, x - cx), cy, cz, lane)
            inside = 0 <= x - cx < LAYERS
            value = moved(second(i, x - cx), cy, cz) if inside else zero
            groups[cx] = groups[cx] + jnp.where(open_path, value, second(OPPOSITES[i], x))
        number = jnp.where(fluid, groups[1] - groups[-1], 0.0)[0:COLUMNS]
        density = jnp.where(fluid, groups[0] + groups[1] + groups[-1], 1.0)[0:COLUMNS]
        if x in (0, LAYERS - 1):
            planes[place(SLOT[x]), :] = number
            planes[place(SLOT[x] + 4), :] = density
        else:
            planes[place(SLOT[x]), :] = number / density
    for slot, ids, x, target in ((6, X_DOWN, 0, -1), (7, X_UP, LAYERS - 1, LAYERS)):
        total = zero
        for i in ids:
            _, cy, cz = VELOCITIES[i]
            open_path = fluid_moved(source(MASK, x), cy, cz, lane)
            total = total + jnp.where(open_path, moved(second(i, x), cy, cz), 0.0)
        total = jnp.where(source(MASK, target) > 0, total, 0.0)
        planes[place(slot), :] = total[0:COLUMNS]
    turned = jnp.transpose(planes[...])
    start = 4 * FIRST_X
    out[0 : HEIGHT - start, :] = turned[start:]
    out[HEIGHT - start :, :] = turned[:start]


def split(value):
    high = value.astype(jnp.bfloat16)
    return high, (value - high.astype(jnp.float32)).astype(jnp.bfloat16)


def dot(a, b):
    return jnp.dot(a, b, preferred_element_type=jnp.float32)


def times_split(stacked, value):
    high, low = split(value)
    count = stacked.shape[0] // 2
    both = dot(stacked, high)
    return both[:count] + (both[count:] + dot(stacked[:count], low))


def split_times(value, high, low):
    stacked = jnp.concatenate(split(value), axis=0)
    count = value.shape[0]
    both = dot(stacked, high)
    return both[:count] + (both[count:] + dot(stacked[:count], low))


def along_x_kernel(got, table, out):
    lane = lax.broadcasted_iota(jnp.int32, (DEVICES_X, HEIGHT), 1)
    within = lambda slot: (lane >= slot * COLUMNS) & (lane < (slot + 1) * COLUMNS)
    speeds = []
    for y in range(4):
        own = got[pl.ds(y, DEVICES_X, stride=4), :]
        from_left = pltpu.roll(own, 1, 0)
        from_right = pltpu.roll(own, DEVICES_X - 1, 0)
        total = own + jnp.where(within(0), pltpu.roll(from_left, 16, 1), 0.0)
        total = total + jnp.where(within(4), pltpu.roll(from_left, 80, 1), 0.0)
        total = total - jnp.where(within(1), pltpu.roll(from_right, 48, 1), 0.0)
        total = total + jnp.where(within(5), pltpu.roll(from_right, 112, 1), 0.0)
        density = jnp.where(lane < 2 * COLUMNS, pltpu.roll(total, 64, 1), 1.0)
        speeds.append(total / density)
    blocks = []
    for x in range(4):
        block = jnp.zeros((DEVICES_X, HEIGHT), jnp.float32)
        for y in range(4):
            piece = pltpu.roll(speeds[y], (COLUMNS * (y - SLOT[x])) % HEIGHT, 1)
            block = jnp.where(within(y), piece, block)
        blocks.append(block)
    blocks += [pltpu.roll(block, 64, 1) for block in blocks]
    lines = jnp.concatenate(blocks, axis=0)
    result = times_split(table[...], lines)
    for r in range(4):
        out[pl.ds(r, DEVICES_Z, stride=4), :] = result[32 * r : 32 * r + 32, :]


def along_z_kernel(got, one, twist_cos, twist_sin, two_high, two_low, out):
    rows = [got[pl.ds(r, DEVICES_Z, stride=4), :] for r in range(4)]
    lines = jnp.concatenate(
        [
            jnp.concatenate([rows[0], rows[1]], axis=1),
            jnp.concatenate([rows[2], rows[3]], axis=1),
        ],
        axis=0,
    )
    inner = times_split(one[...], lines)
    real, imag = inner[0:32], inner[32:64]
    cosine, sine = twist_cos[...], twist_sin[...]
    turned = jnp.concatenate([real * cosine + imag * sine, imag * cosine - real * sine], axis=0)
    both = split_times(turned, two_high[...], two_low[...])
    outer_real = both[0:32, 0:256] + both[32:64, 256:512]
    outer_imag = both[32:64, 0:256] - both[0:32, 256:512]
    for c, value in enumerate((outer_real, outer_imag)):
        columns = jnp.transpose(value)
        for quad in range(4):
            parts = [columns[16 * k : 16 * k + 16] for k in range(4 * quad, 4 * quad + 4)]
            tile = jnp.concatenate(parts, axis=1)
            for y in range(4):
                out[c, y, :, 128 * quad : 128 * quad + 128] = tile[4 * y : 4 * y + 4]


def halves(table):
    table = np.asarray(table, np.float32)
    high = table.astype(ml_dtypes.bfloat16)
    low = (table - high.astype(np.float32)).astype(ml_dtypes.bfloat16)
    return high, low


def x_table():
    part, pair, block = np.meshgrid(np.arange(2), np.arange(2), np.arange(32), indexing="ij")
    odd, inner, outer = np.meshgrid(np.arange(2), np.arange(4), np.arange(32), indexing="ij")
    kx = (4 * (np.asarray(ORDER_Z)[block]) + 2 * pair).reshape(-1, 1) + odd.reshape(1, -1)
    x = (4 * ((outer + FIRST_X) % 32) + inner).reshape(1, -1)
    angle = 2.0 * np.pi * ((kx * x) % NX) / NX
    scale = 1.0 / (math.sqrt(NX * NZ) * SPEED_UNIT)
    table = halves(np.where(part.reshape(-1, 1) == 0, np.cos(angle), -np.sin(angle)) * scale)
    return np.concatenate(table, axis=0)


def z_tables():
    k, b = np.meshgrid(np.arange(32), np.asarray(ORDER_Z), indexing="ij")
    angle = 2.0 * np.pi * ((k * b) % 32) / 32
    one = np.block([[np.cos(angle), np.sin(angle)], [-np.sin(angle), np.cos(angle)]])
    angle = 2.0 * np.pi * (np.arange(32)[:, None] * (np.arange(256) % 16 + SHIFT)[None, :]) / NZ
    pair, odd, y, z = (v.reshape(-1, 1) for v in np.unravel_index(np.arange(256), (2, 2, 4, 16)))
    k_out, y_out, kx_out = (v.reshape(1, -1) for v in np.unravel_index(np.arange(256), (16, 4, 4)))
    same = (y == y_out) & (2 * pair + odd == kx_out)
    turn = 2.0 * np.pi * (((z + SHIFT) * k_out) % 16) / 16
    two = np.concatenate([same * np.cos(turn), same * np.sin(turn)], axis=1)
    return (
        np.concatenate(halves(one), axis=0),
        np.cos(angle).astype(np.float32),
        np.sin(angle).astype(np.float32),
        *halves(two),
    )


def call(kernel, name, *shapes, scratch=(), in_specs=None):
    outs = tuple(jax.ShapeDtypeStruct(shape, jnp.float32) for shape in shapes)
    return pl.pallas_call(
        kernel,
        out_shape=outs if len(outs) > 1 else outs[0],
        **({} if in_specs is None else {"in_specs": in_specs}),
        scratch_shapes=[
            pltpu.VMEM(shape, jnp.float32) if isinstance(shape, tuple) else shape
            for shape in scratch
        ],
        compiler_params=PARAMS,
        name=name,
    )


def near_pairs(count):
    return [(i, i ^ 1) for i in range(count)]


def far_pairs(count):
    return [(i, (i + (1 if i % 2 else -1)) % count) for i in range(count)]


def swap(near, far, axis, count):
    near = lax.ppermute(near, axis, near_pairs(count))
    far = lax.ppermute(far, axis, far_pairs(count))
    return near, far


def exchange(rows, axis, members):
    return lax.all_to_all(
        rows, axis, split_axis=0, concat_axis=0, tiled=True, axis_index_groups=[members]
    )


def shards(populations, fluid_mask):
    block = (LAYERS, COLUMNS, HEIGHT)
    z_edge = (Z_ROWS, HEIGHT)
    x_edge = (X_ROWS, HEIGHT)
    relaxed, edge = call(
        collide_kernel,
        "collide",
        (20,) + block,
        z_edge,
        in_specs=[pl.BlockSpec(memory_space=pltpu.HBM)] * 2,
        scratch=(
            (19,) + block,
            pltpu.VMEM(block, jnp.int32),
            pltpu.SemaphoreType.DMA((LAYERS + 1,)),
        ),
    )(
        pltpu.with_memory_space_constraint(populations, pltpu.HBM),
        pltpu.with_memory_space_constraint(fluid_mask, pltpu.HBM),
    )
    beyond = lax.ppermute(edge, "gz", [(i, (i - 1) % DEVICES_Z) for i in range(DEVICES_Z)])
    far, near = call(face_kernel, "faces", x_edge, x_edge, scratch=(x_edge, x_edge))(relaxed, beyond)
    x_near, x_far = swap(near, far, "gx", DEVICES_X)
    ring_block = (LAYERS, RING, HEIGHT)
    first, inner = call(inner_kernel, "inner", (20,) + ring_block, (19, 2, RING, HEIGHT))(
        relaxed, beyond
    )
    sums = call(
        outer_kernel,
        "outer",
        (HEIGHT, HEIGHT),
        scratch=((19, 2, RING, HEIGHT), (HEIGHT, HEIGHT), x_edge, x_edge),
    )(first, inner, x_far, x_near)
    lines = exchange(sums, "gx", [(FIRST_X + i) % DEVICES_X for i in range(DEVICES_X)])
    spectrum = call(along_x_kernel, "along_x", (4 * DEVICES_Z, HEIGHT))(lines, x_table())
    spectrum = exchange(spectrum, "gz", list(ORDER_Z))
    return call(along_z_kernel, "along_z", (2, 4, 4, NZ))(spectrum, *z_tables())


def solution(mesh):
    placed = (P(None, "gx", "gz", None), P("gx", "gz", None))
    return jax.shard_map(
        shards, mesh=mesh, in_specs=placed, out_specs=P(None, "gx", "gz", None), check_vma=False
    )
```

```python
import math

import jax
import jax.numpy as jnp
import ml_dtypes
import numpy as np
from jax import lax
from jax.experimental import pallas as pl
from jax.experimental.pallas import tpu as pltpu
from jax.sharding import PartitionSpec as P

VELOCITIES = (
    (0, 0, 0),
    (1, 0, 0),
    (-1, 0, 0),
    (0, 1, 0),
    (0, -1, 0),
    (0, 0, 1),
    (0, 0, -1),
    (1, 1, 0),
    (-1, -1, 0),
    (1, -1, 0),
    (-1, 1, 0),
    (1, 0, 1),
    (-1, 0, -1),
    (1, 0, -1),
    (-1, 0, 1),
    (0, 1, 1),
    (0, -1, -1),
    (0, 1, -1),
    (0, -1, 1),
)
WEIGHTS = (1.0 / 3.0,) + (1.0 / 18.0,) * 6 + (1.0 / 36.0,) * 12
OPPOSITES = (0, 2, 1, 4, 3, 6, 5, 8, 7, 10, 9, 12, 11, 14, 13, 16, 15, 18, 17)
OMEGA = 1.0 / 0.6
BODY_FORCE = 0.0001
SPEED_UNIT = 0.05

DEVICES_X = 32
DEVICES_Z = 32
LAYERS = 4
COLUMNS = 16
HEIGHT = 128
NX = 128
NZ = 512
MASK = 19
RING = 24
FIRST_X = 18
SLOT = (0, 2, 3, 1)
ORDER_Z = tuple((21 + i) % 32 for i in range(32))

X_UP = tuple(i for i in range(19) if VELOCITIES[i][0] == 1)
X_DOWN = tuple(i for i in range(19) if VELOCITIES[i][0] == -1)
Z_UP = tuple(i for i in range(19) if VELOCITIES[i][2] == 1)
Z_DOWN = tuple(i for i in range(19) if VELOCITIES[i][2] == -1)
SHIFT = 2
DEPTH = tuple(4 if i in Z_DOWN + (MASK,) else 3 for i in range(20))
Z_START = tuple(LAYERS * sum(DEPTH[:i]) for i in range(20))
Z_ROWS = LAYERS * sum(DEPTH)
X_ROWS = 6 * RING

PARAMS = pltpu.CompilerParams(vmem_limit_bytes=32 * 1024 * 1024)


def relax(current, fluid):
    plus = lambda ids: sum(current[i] for i in ids[1:]) + current[ids[0]]
    right, left = plus(X_UP), plus(X_DOWN)
    rho = plus(tuple(i for i in range(19) if VELOCITIES[i][0] == 0)) + right + left
    flow_x = right - left
    flow_y = plus(tuple(i for i in range(19) if VELOCITIES[i][1] == 1)) - plus(
        tuple(i for i in range(19) if VELOCITIES[i][1] == -1)
    )
    flow_z = plus(Z_UP) - plus(Z_DOWN)
    inverse = 1.0 / rho
    ux, uy, uz = flow_x * inverse, flow_y * inverse, flow_z * inverse
    scaled = rho * OMEGA
    rest = scaled * (1.0 - 1.5 * (ux * ux + uy * uy + uz * uz))
    odd_scale = 3.0 * scaled
    even_scale = 4.5 * scaled
    push = (3.0 * BODY_FORCE) * rho
    out = [None] * 19
    keep = 1.0 - OMEGA
    out[0] = jnp.where(fluid, keep * current[0] + WEIGHTS[0] * rest, current[0])
    for i in range(1, 19, 2):
        cx, cy, cz = VELOCITIES[i]
        parts = [u if c == 1 else -u for c, u in ((cx, ux), (cy, uy), (cz, uz)) if c]
        along = parts[0] if len(parts) == 1 else parts[0] + parts[1]
        even = WEIGHTS[i] * (rest + even_scale * (along * along))
        odd = odd_scale * along
        if cx:
            odd = odd + push if cx == 1 else odd - push
        odd = WEIGHTS[i] * odd
        j = OPPOSITES[i]
        out[i] = jnp.where(fluid, keep * current[i] + (even + odd), current[i])
        out[j] = jnp.where(fluid, keep * current[j] + (even - odd), current[j])
    return out


def even_index(axis):
    return lax.axis_index(axis) % 2 == 0


def collide_tile(z, pop, mask, relaxed, edge, held, solid, arrivals):
    rows = slice(z, z + 8)
    copies = [
        pltpu.make_async_copy(pop.at[:, x, rows], held.at[:, x], arrivals.at[x])
        for x in range(LAYERS)
    ]
    copies.append(pltpu.make_async_copy(mask.at[:, rows], solid, arrivals.at[LAYERS]))
    for copy in copies[::-1]:
        copy.start()
    copies[LAYERS].wait()
    for x in range(LAYERS)[::-1]:
        copies[x].wait()
        fluid_here = solid[x].astype(jnp.float32)
        out = relax([held[i, x] for i in range(19)], fluid_here > 0) + [fluid_here]
        for i in range(20):
            relaxed[i, x] = out[i]
            if edge is not None:
                start = Z_START[i] + x * DEPTH[i]
                edge[start : start + DEPTH[i], :] = out[i][0 : DEPTH[i]]


def low_kernel(pop, mask, relaxed, edge, held, solid, arrivals):
    collide_tile(0, pop, mask, relaxed, edge, held, solid, arrivals)


def high_kernel(pop, mask, relaxed, held, solid, arrivals):
    collide_tile(8, pop, mask, relaxed, None, held, solid, arrivals)


def widen(target, i, x, low, high, beyond):
    start = Z_START[i] + x * DEPTH[i]
    target[0:8] = low[i, x]
    target[8:COLUMNS] = high[i, x]
    target[COLUMNS:RING] = jnp.zeros((RING - COLUMNS, HEIGHT), jnp.float32)
    target[COLUMNS : COLUMNS + DEPTH[i]] = beyond[start : start + DEPTH[i], :]
    target[...] = pltpu.roll(target[...], RING - SHIFT, 0)


def face_kernel(low, high, beyond, far, near, right, left):
    for send, ids, x in ((right, X_UP, LAYERS - 1), (left, X_DOWN, 0)):
        for v, i in enumerate(ids + (MASK,)):
            widen(send.at[v * RING : (v + 1) * RING], i, x, low, high, beyond)
    even = even_index("gx")
    near[...] = jnp.where(even, right[...], left[...])
    far[...] = jnp.where(even, left[...], right[...])


def moved(value, cy, cz):
    if cz:
        value = pltpu.roll(value, cz % RING, 0)
    if cy:
        value = pltpu.roll(value, cy % HEIGHT, 1)
    return value


def fluid_moved(value, cy, cz, lane):
    value = moved(value, cy, cz)
    if cy:
        value = jnp.where(lane == (0 if cy == 1 else HEIGHT - 1), 0.0, value)
    return value > 0


def advance(x, source, own, store):
    lane = lax.broadcasted_iota(jnp.int32, (RING, HEIGHT), 1)
    fluid = source(MASK, x) > 0
    arrived = [own(0, x)]
    for i in range(1, 19):
        cx, cy, cz = VELOCITIES[i]
        open_path = fluid_moved(source(MASK, x - cx), cy, cz, lane)
        value = jnp.where(open_path, moved(source(i, x - cx), cy, cz), own(OPPOSITES[i], x))
        arrived.append(jnp.where(fluid, value, own(i, x)))
    for i, value in enumerate(relax(arrived, fluid)):
        store[i] = value


def inner_kernel(low, high, beyond, first, second):
    for i in range(20):
        for x in range(LAYERS):
            widen(first.at[i, x], i, x, low, high, beyond)
    read = lambda i, x: first[i, x]
    for x in range(1, LAYERS - 1):
        advance(x, read, read, second.at[:, x - 1])


def outer_kernel(first, inner, x_far, x_near, out, outer, planes, from_left, from_right):
    even = even_index("gx")
    from_left[...] = jnp.where(even, x_far[...], x_near[...])
    from_right[...] = jnp.where(even, x_near[...], x_far[...])
    lane = lax.broadcasted_iota(jnp.int32, (RING, HEIGHT), 1)

    def face(ref, ids, i):
        v = 5 if i == MASK else ids.index(i)
        return ref[v * RING : (v + 1) * RING, :]

    def source(i, x):
        if x < 0:
            return face(from_left, X_UP, i)
        if x >= LAYERS:
            return face(from_right, X_DOWN, i)
        return first[i, x]

    def second(i, x):
        return outer[i, x // (LAYERS - 1)] if x in (0, LAYERS - 1) else inner[i, x - 1]

    for x in (0, LAYERS - 1):
        advance(x, source, source, outer.at[:, x // (LAYERS - 1)])

    zero = jnp.zeros((RING, HEIGHT), jnp.float32)
    place = lambda slot: slice(slot * COLUMNS, (slot + 1) * COLUMNS)
    for x in range(LAYERS):
        fluid = source(MASK, x) > 0
        groups = {-1: zero, 0: second(0, x), 1: zero}
        for i in range(1, 19):
            cx, cy, cz = VELOCITIES[i]
            open_path = fluid_moved(source(MASK, x - cx), cy, cz, lane)
            inside = 0 <= x - cx < LAYERS
            value = moved(second(i, x - cx), cy, cz) if inside else zero
            groups[cx] = groups[cx] + jnp.where(open_path, value, second(OPPOSITES[i], x))
        number = jnp.where(fluid, groups[1] - groups[-1], 0.0)[0:COLUMNS]
        density = jnp.where(fluid, groups[0] + groups[1] + groups[-1], 1.0)[0:COLUMNS]
        if x in (0, LAYERS - 1):
            planes[place(SLOT[x]), :] = number
            planes[place(SLOT[x] + 4), :] = density
        else:
            planes[place(SLOT[x]), :] = number / density
    for slot, ids, x, target in ((6, X_DOWN, 0, -1), (7, X_UP, LAYERS - 1, LAYERS)):
        total = zero
        for i in ids:
            _, cy, cz = VELOCITIES[i]
            open_path = fluid_moved(source(MASK, x), cy, cz, lane)
            total = total + jnp.where(open_path, moved(second(i, x), cy, cz), 0.0)
        total = jnp.where(source(MASK, target) > 0, total, 0.0)
        planes[place(slot), :] = total[0:COLUMNS]
    turned = jnp.transpose(planes[...])
    start = 4 * FIRST_X
    out[0 : HEIGHT - start, :] = turned[start:]
    out[HEIGHT - start :, :] = turned[:start]


def split(value):
    high = value.astype(jnp.bfloat16)
    return high, (value - high.astype(jnp.float32)).astype(jnp.bfloat16)


def dot(a, b):
    return jnp.dot(a, b, preferred_element_type=jnp.float32)


def times_split(stacked, value):
    high, low = split(value)
    count = stacked.shape[0] // 2
    both = dot(stacked, high)
    return both[:count] + (both[count:] + dot(stacked[:count], low))


def split_times(value, high, low):
    stacked = jnp.concatenate(split(value), axis=0)
    count = value.shape[0]
    both = dot(stacked, high)
    return both[:count] + (both[count:] + dot(stacked[:count], low))


def along_x_kernel(got, table, out):
    lane = lax.broadcasted_iota(jnp.int32, (DEVICES_X, HEIGHT), 1)
    within = lambda slot: (lane >= slot * COLUMNS) & (lane < (slot + 1) * COLUMNS)
    speeds = []
    for y in range(4):
        own = got[pl.ds(y, DEVICES_X, stride=4), :]
        from_left = pltpu.roll(own, 1, 0)
        from_right = pltpu.roll(own, DEVICES_X - 1, 0)
        total = own + jnp.where(within(0), pltpu.roll(from_left, 16, 1), 0.0)
        total = total + jnp.where(within(4), pltpu.roll(from_left, 80, 1), 0.0)
        total = total - jnp.where(within(1), pltpu.roll(from_right, 48, 1), 0.0)
        total = total + jnp.where(within(5), pltpu.roll(from_right, 112, 1), 0.0)
        density = jnp.where(lane < 2 * COLUMNS, pltpu.roll(total, 64, 1), 1.0)
        speeds.append(total / density)
    blocks = []
    for x in range(4):
        block = jnp.zeros((DEVICES_X, HEIGHT), jnp.float32)
        for y in range(4):
            piece = pltpu.roll(speeds[y], (COLUMNS * (y - SLOT[x])) % HEIGHT, 1)
            block = jnp.where(within(y), piece, block)
        blocks.append(block)
    blocks += [pltpu.roll(block, 64, 1) for block in blocks]
    lines = jnp.concatenate(blocks, axis=0)
    result = times_split(table[...], lines)
    for r in range(4):
        out[pl.ds(r, DEVICES_Z, stride=4), :] = result[32 * r : 32 * r + 32, :]


def along_z_kernel(got, one, twist_cos, twist_sin, two_high, two_low, out):
    rows = [got[pl.ds(r, DEVICES_Z, stride=4), :] for r in range(4)]
    lines = jnp.concatenate(
        [
            jnp.concatenate([rows[0], rows[1]], axis=1),
            jnp.concatenate([rows[2], rows[3]], axis=1),
        ],
        axis=0,
    )
    inner = times_split(one[...], lines)
    real, imag = inner[0:32], inner[32:64]
    cosine, sine = twist_cos[...], twist_sin[...]
    turned = jnp.concatenate([real * cosine + imag * sine, imag * cosine - real * sine], axis=0)
    both = split_times(turned, two_high[...], two_low[...])
    outer_real = both[0:32, 0:256] + both[32:64, 256:512]
    outer_imag = both[32:64, 0:256] - both[0:32, 256:512]
    for c, value in enumerate((outer_real, outer_imag)):
        columns = jnp.transpose(value)
        for quad in range(4):
            parts = [columns[16 * k : 16 * k + 16] for k in range(4 * quad, 4 * quad + 4)]
            tile = jnp.concatenate(parts, axis=1)
            for y in range(4):
                out[c, y, :, 128 * quad : 128 * quad + 128] = tile[4 * y : 4 * y + 4]


def halves(table):
    table = np.asarray(table, np.float32)
    high = table.astype(ml_dtypes.bfloat16)
    low = (table - high.astype(np.float32)).astype(ml_dtypes.bfloat16)
    return high, low


def x_table():
    part, pair, block = np.meshgrid(np.arange(2), np.arange(2), np.arange(32), indexing="ij")
    odd, inner, outer = np.meshgrid(np.arange(2), np.arange(4), np.arange(32), indexing="ij")
    kx = (4 * (np.asarray(ORDER_Z)[block]) + 2 * pair).reshape(-1, 1) + odd.reshape(1, -1)
    x = (4 * ((outer + FIRST_X) % 32) + inner).reshape(1, -1)
    angle = 2.0 * np.pi * ((kx * x) % NX) / NX
    scale = 1.0 / (math.sqrt(NX * NZ) * SPEED_UNIT)
    table = halves(np.where(part.reshape(-1, 1) == 0, np.cos(angle), -np.sin(angle)) * scale)
    return np.concatenate(table, axis=0)


def z_tables():
    k, b = np.meshgrid(np.arange(32), np.asarray(ORDER_Z), indexing="ij")
    angle = 2.0 * np.pi * ((k * b) % 32) / 32
    one = np.block([[np.cos(angle), np.sin(angle)], [-np.sin(angle), np.cos(angle)]])
    angle = 2.0 * np.pi * (np.arange(32)[:, None] * (np.arange(256) % 16 + SHIFT)[None, :]) / NZ
    pair, odd, y, z = (v.reshape(-1, 1) for v in np.unravel_index(np.arange(256), (2, 2, 4, 16)))
    k_out, y_out, kx_out = (v.reshape(1, -1) for v in np.unravel_index(np.arange(256), (16, 4, 4)))
    same = (y == y_out) & (2 * pair + odd == kx_out)
    turn = 2.0 * np.pi * (((z + SHIFT) * k_out) % 16) / 16
    two = np.concatenate([same * np.cos(turn), same * np.sin(turn)], axis=1)
    return (
        np.concatenate(halves(one), axis=0),
        np.cos(angle).astype(np.float32),
        np.sin(angle).astype(np.float32),
        *halves(two),
    )


def call(kernel, name, *shapes, scratch=(), in_specs=None):
    outs = tuple(jax.ShapeDtypeStruct(shape, jnp.float32) for shape in shapes)
    return pl.pallas_call(
        kernel,
        out_shape=outs if len(outs) > 1 else outs[0],
        **({} if in_specs is None else {"in_specs": in_specs}),
        scratch_shapes=[
            pltpu.VMEM(shape, jnp.float32) if isinstance(shape, tuple) else shape
            for shape in scratch
        ],
        compiler_params=PARAMS,
        name=name,
    )


def near_pairs(count):
    return [(i, i ^ 1) for i in range(count)]


def far_pairs(count):
    return [(i, (i + (1 if i % 2 else -1)) % count) for i in range(count)]


def swap(near, far, axis, count):
    near = lax.ppermute(near, axis, near_pairs(count))
    far = lax.ppermute(far, axis, far_pairs(count))
    return near, far


def exchange(rows, axis, members):
    return lax.all_to_all(
        rows, axis, split_axis=0, concat_axis=0, tiled=True, axis_index_groups=[members]
    )


def shards(populations, fluid_mask):
    z_edge = (Z_ROWS, HEIGHT)
    x_edge = (X_ROWS, HEIGHT)
    tile = (LAYERS, 8, HEIGHT)
    inputs = (
        pltpu.with_memory_space_constraint(populations, pltpu.HBM),
        pltpu.with_memory_space_constraint(fluid_mask, pltpu.HBM),
    )
    options = dict(
        in_specs=[pl.BlockSpec(memory_space=pltpu.HBM)] * 2,
        scratch=(
            (19,) + tile,
            pltpu.VMEM(tile, jnp.int32),
            pltpu.SemaphoreType.DMA((LAYERS + 1,)),
        ),
    )
    low, edge = call(low_kernel, "low", (20,) + tile, z_edge, **options)(*inputs)
    beyond = lax.ppermute(edge, "gz", [(i, (i - 1) % DEVICES_Z) for i in range(DEVICES_Z)])
    high = call(high_kernel, "high", (20,) + tile, **options)(*inputs)
    far, near = call(face_kernel, "faces", x_edge, x_edge, scratch=(x_edge, x_edge))(
        low, high, beyond
    )
    x_near, x_far = swap(near, far, "gx", DEVICES_X)
    ring_block = (LAYERS, RING, HEIGHT)
    first, inner = call(inner_kernel, "inner", (20,) + ring_block, (19, 2, RING, HEIGHT))(
        low, high, beyond
    )
    sums = call(
        outer_kernel,
        "outer",
        (HEIGHT, HEIGHT),
        scratch=((19, 2, RING, HEIGHT), (HEIGHT, HEIGHT), x_edge, x_edge),
    )(first, inner, x_far, x_near)
    lines = exchange(sums, "gx", [(FIRST_X + i) % DEVICES_X for i in range(DEVICES_X)])
    spectrum = call(along_x_kernel, "along_x", (4 * DEVICES_Z, HEIGHT))(lines, x_table())
    spectrum = exchange(spectrum, "gz", list(ORDER_Z))
    return call(along_z_kernel, "along_z", (2, 4, 4, NZ))(spectrum, *z_tables())


def solution(mesh):
    placed = (P(None, "gx", "gz", None), P("gx", "gz", None))
    return jax.shard_map(
        shards, mesh=mesh, in_specs=placed, out_specs=P(None, "gx", "gz", None), check_vma=False
    )
```
